512 devices in a mesh: row: 16 (over x, z_hi, core), col: 32 (over y, z_lo).
Axes of the slice: x: 4, y: 8, z: 8 (z_hi: 2, z_lo: 4; z = z_hi * 4 + z_lo), core: 2. Of those that a mesh axis runs over, the one named last changes fastest.
Arguments:
- inverse_tiles: bfloat16 [4, 16, 256, 2, 32, 256], P(None, 'row', None, None, 'col'), may hold values from -6 to 6
- lower_panels: bfloat16 [3, 4, 16, 256, 256], P(None, None, 'row', 'col'), may hold values from -0.046875 to 0.046875
- diag_inverse: float32 [3, 256, 256], replicated, may hold values from -6 to 6
- selected: int32 [3, 64], replicated, may hold values 0 or 1
Outputs:
- panel_inverse: float32 [3, 4, 16, 256, 256], P(None, None, 'row', 'col')
- diagonal_inverse: float32 [3, 256, 256], replicated
The draws below stay inside these ranges and needn't reach their ends.
All inputs are finite; a program needn't handle non-finite values.
Results may differ from the reference program's by a relative error of at most 0.0003.
Values may be sent and summed in bfloat16 or wider, within the bound.
No kernel may reach another device: no remote copies, remote signals or barrier semaphores. Data moves between devices by JAX's collectives and lax.ppermute only.
A program may use at most 64 MiB of HBM per device.

```python
import jax
import jax.numpy as jnp
from jax import lax

W = 256
KS = 3
RB = 4
CB = 2
NB = 64
N_ROW = 16
N_COL = 32


def plant(drawn, key, least, high):
    dims = drawn.shape
    index_at = [jax.random.randint(jax.random.fold_in(key, axis), (), 0, dims[axis]) for axis in range(len(dims))]
    drawn = drawn.at[tuple(index_at)].set(least)
    longest = dims.index(max(dims))
    index_at[longest] = (index_at[longest] + 1) % dims[longest]
    return drawn.at[tuple(index_at)].set(high)


def level_of(key, extent, split, smallest, largest):
    loudness, own = 1.0, jax.random.fold_in(key, 6)
    for axis_at, blocks in split:
        draws = jnp.exp(jax.random.uniform(jax.random.fold_in(own, axis_at), (blocks,), jnp.float32, smallest / len(split), largest / len(split)))
        loudness = loudness * jnp.repeat(draws, extent[axis_at] // blocks).reshape([-1 if axis == axis_at else 1 for axis in range(len(extent))])
    return loudness


def centred(rng, dims, spread, reach, split=(), kind=jnp.bfloat16):
    entries = jax.random.normal(rng, dims, jnp.float32) * spread
    if len(split) > 0:
        entries = level_of(rng, dims, split, -0.22, 0.18) * entries
    return jnp.clip(entries, min=-reach, max=reach).astype(kind)


def setup_inputs(seed: int = 0) -> dict:
    keys = jax.random.split(jax.random.key(seed), 5)
    return {
        "inverse_tiles": centred(keys[0], (RB, N_ROW, W, CB, N_COL, W), 1.0, 6.0, ((1, 16), (4, 32))),
        "lower_panels": centred(keys[1], (KS, RB, N_ROW, W, W), (RB * N_ROW * W) ** -0.5, 0.046875, ((2, 16), (3, 32))),
        "diag_inverse": centred(keys[2], (KS, W, W), 1.0, 6.0, (), jnp.float32),
        "selected": plant((jax.random.randint(keys[3], (KS, NB), 0, 8) < 7).astype(jnp.int32), jax.random.fold_in(keys[3], 1), 0, 1),
    }


def reference(inverse_tiles, lower_panels, diag_inverse, selected):
    matrix_order = RB * N_ROW * W
    full_matrix = inverse_tiles.reshape(matrix_order, CB, N_COL, W)
    row_keep = jnp.repeat(selected.astype(jnp.float32), W, axis=1)
    panels = []
    diagonals = []
    for member in range(KS):
        lower_rows = lower_panels[member].reshape(matrix_order, W)
        masked = (lower_rows.astype(jnp.float32) * row_keep[member][:, None]).astype(jnp.bfloat16)
        masked = masked.reshape(CB, N_COL, W, W)

        def add_column(column, running):
            col_block = lax.dynamic_index_in_dim(full_matrix, column, 2, keepdims=False).reshape(matrix_order, CB * W)
            panel_part = lax.dynamic_index_in_dim(masked, column, 1, keepdims=False).reshape(CB * W, W)
            partial_value = jnp.dot(col_block, panel_part, preferred_element_type=jnp.float32)
            return running + partial_value

        summed = lax.fori_loop(0, N_COL, add_column, jnp.zeros((matrix_order, W), jnp.float32))
        panel_block = -summed * row_keep[member][:, None]
        diag_block = diag_inverse[member] - jnp.dot(lower_rows.astype(jnp.float32).T, panel_block, precision=lax.Precision.HIGHEST)
        panels.append(panel_block.reshape(RB, N_ROW, W, W))
        diagonals.append(diag_block)
    return jnp.stack(panels), jnp.stack(diagonals)
```

```python
import functools

import jax
import jax.numpy as jnp
from jax import lax
from jax.experimental import pallas as pl
from jax.experimental.pallas import tpu as pltpu
from jax.sharding import Mesh, PartitionSpec as P

KS, RB, W = 3, 4, 256
ROW = ("x", "zh", "core")
COL = ("y", "zl")
CHIPS = ("y", "zl", "x", "zh")
STEPS = 32760.0
FLOOR = 1e-36


def product_kernel(tile_ref, cols_ref, out_ref):
    lane = lax.broadcasted_iota(jnp.int32, (W, 128), 1)
    codes = jnp.zeros((W, 128), jnp.float32)
    for r in range(RB):
        part = jnp.dot(
            tile_ref[r * W : (r + 1) * W, :], cols_ref[...], preferred_element_type=jnp.float32
        )
        for k in range(KS):
            block = part[:, k * W : (k + 1) * W]
            peak = jnp.maximum(jnp.max(jnp.abs(block), axis=1, keepdims=True), FLOOR)
            code = jnp.ceil(jnp.log2(peak) * 8.0 + 0.01)
            whole = jnp.round(block * (jnp.exp2(code * -0.125) * STEPS))
            whole = whole.astype(jnp.int32).astype(jnp.int16)
            for half in range(2):
                out_ref[:, r * 6 + k * 2 + half] = whole[:, half * 128 : (half + 1) * 128].reshape(
                    32, 8, 128
                )
            codes = jnp.where(lane == r * KS + k, code, codes)
    out_ref[:, 24] = codes.astype(jnp.int32).astype(jnp.int16).reshape(32, 8, 128)


def sum_kernel(parts_ref, lower_ref, keep_ref, panel_ref, diag_ref):
    scales = jnp.exp2(parts_ref[:, 24].astype(jnp.float32) * 0.125) * (1.0 / STEPS)
    for k in range(KS):
        rows = []
        for r in range(RB):
            at = r * KS + k
            scale = scales[:, :, at : at + 1]
            halves = []
            for half in range(2):
                part = parts_ref[:, r * 6 + k * 2 + half].astype(jnp.float32)
                halves.append(jnp.sum(part * scale, axis=0))
            block = -(jnp.concatenate(halves, axis=1) * keep_ref[k, r])
            panel_ref[k, r] = block
            rows.append(block)
        panel = jnp.concatenate(rows, axis=0)
        high = panel.astype(jnp.bfloat16)
        rest = panel - high.astype(jnp.float32)
        middle = rest.astype(jnp.bfloat16)
        low = (rest - middle.astype(jnp.float32)).astype(jnp.bfloat16)
        lower = lower_ref[k].astype(jnp.float32).reshape(RB * 8, W).astype(jnp.bfloat16)
        left = jnp.concatenate([lower, lower, lower], axis=0)
        right = jnp.concatenate([high, middle, low], axis=0)
        diag_ref[k * W : (k + 1) * W, :] = lax.dot_general(
            left, right, (((0,), (0,)), ((), ())), preferred_element_type=jnp.float32
        )


def vmem(count):
    return [pl.BlockSpec(memory_space=pltpu.VMEM)] * count


def per_device(inverse_tiles, lower_panels, diag_inverse, selected):
    core = lax.axis_index("core")
    row = lax.axis_index(ROW)
    keep = lax.dynamic_index_in_dim(
        selected.reshape(KS, RB, 16), row, axis=2, keepdims=False
    ).astype(jnp.float32)
    lower = lower_panels[:, :, 0]
    masked = lower * keep.astype(jnp.bfloat16)[:, :, None, None]
    pieces = masked.reshape(KS, 2, 2, 8, W).transpose(3, 1, 2, 0, 4).reshape(16, 2 * KS, W)
    spread = lax.all_to_all(pieces, ROW, 0, 0, tiled=True)
    spread = spread.reshape(16, 2, KS * W).transpose(1, 0, 2).reshape(32, 1, KS * W)
    repeated = jnp.broadcast_to(spread, (32, 8, KS * W)).reshape(256, KS * W)
    half = lax.all_to_all(repeated, CHIPS, 0, 0, tiled=True)
    columns = lax.all_gather(half, "core", axis=0, tiled=True)
    tile = inverse_tiles.reshape(RB * W, 2 * W)
    parts = pl.pallas_call(
        product_kernel,
        out_shape=jax.ShapeDtypeStruct((32, 25, 8, 128), jnp.int16),
        in_specs=vmem(2),
        out_specs=pl.BlockSpec(memory_space=pltpu.VMEM),
        name="product",
    )(tile, columns)
    parts = lax.all_to_all(parts, COL, 0, 0, tiled=True)
    panel_out, partial_value = pl.pallas_call(
        sum_kernel,
        out_shape=(
            jax.ShapeDtypeStruct((KS, RB, 8, W), jnp.float32),
            jax.ShapeDtypeStruct((KS * W, W), jnp.float32),
        ),
        in_specs=vmem(2) + [pl.BlockSpec(memory_space=pltpu.SMEM)],
        out_specs=tuple(vmem(2)),
        name="total",
    )(parts, lower, keep)
    halves = partial_value.reshape(2, KS * W // 2, W)
    mine = lax.dynamic_index_in_dim(halves, core, 0, keepdims=False)
    other = lax.dynamic_index_in_dim(halves, 1 - core, 0, keepdims=False)
    mine = mine + lax.ppermute(other, "core", [(0, 1), (1, 0)])
    slices = lax.all_to_all(mine.reshape(256, 384), CHIPS, 0, 0, tiled=True)
    total = jnp.sum(slices, axis=0, keepdims=True)
    spread_total = lax.all_to_all(jnp.broadcast_to(total, (256, 384)), CHIPS, 0, 0, tiled=True)
    both = lax.all_gather(spread_total.reshape(KS * W // 2, W), "core", axis=0, tiled=True)
    diagonal = diag_inverse - both.reshape(KS, W, W)
    return (panel_out[:, :, None], diagonal)


def solution(mesh):
    finer = Mesh(mesh.devices.reshape(4, 2, 2, 8, 4), ROW + COL)
    in_specs = (
        P(None, ROW, None, None, COL, None),
        P(None, None, ROW, COL, None),
        P(),
        P(),
    )
    out_specs = (P(None, None, ROW, COL, None), P())
    return jax.shard_map(
        per_device, mesh=finer, in_specs=in_specs, out_specs=out_specs, check_vma=False
    )
```

```python
import jax
import jax.numpy as jnp
from jax import lax
from jax.experimental import pallas as pl
from jax.experimental.pallas import tpu as pltpu
from jax.sharding import Mesh, PartitionSpec as P

KS, RB, W = 3, 4, 256
ROW = ("x", "zh", "core")
COL = ("y", "zl")
PLANE = ("y", "x")
LINE = ("zh", "zl")
STEPS = 32760.0
FLOOR = 1e-36
LIMIT = 24 * 1024 * 1024


def spread_kernel(row_ref, selected_ref, lower_ref, out_ref):
    for k in range(KS):
        for s in range(2):
            for h in range(2):
                r = 2 * s + h
                keep = selected_ref[k, r * 16 + row_ref[0]].astype(jnp.float32)
                block = (lower_ref[k, r].astype(jnp.float32) * keep).astype(jnp.bfloat16)
                for chip in range(8):
                    out_ref[chip * 2 + s, h * KS + k] = block


def product_kernel(tile_ref, cols_ref, out_ref):
    lane = lax.broadcasted_iota(jnp.int32, (W, 128), 1)
    codes = jnp.zeros((W, 128), jnp.float32)
    for k in range(KS):
        first = cols_ref[0, :, k].reshape(W, W)
        second = cols_ref[1, :, k].reshape(W, W)
        columns = jnp.concatenate([first, second], axis=0)
        for r in range(RB):
            block = jnp.dot(
                tile_ref[r * W : (r + 1) * W, :], columns, preferred_element_type=jnp.float32
            )
            peak = jnp.maximum(jnp.max(jnp.abs(block), axis=1, keepdims=True), FLOOR)
            code = jnp.ceil(jnp.log2(peak) * 8.0 + 0.01)
            whole = jnp.round(block * (jnp.exp2(code * -0.125) * STEPS))
            whole = whole.astype(jnp.int32).astype(jnp.int16)
            for half in range(2):
                out_ref[:, r * 6 + k * 2 + half] = whole[:, half * 128 : (half + 1) * 128].reshape(
                    32, 8, 128
                )
            codes = jnp.where(lane == r * KS + k, code, codes)
    out_ref[:, 24] = codes.astype(jnp.int32).astype(jnp.int16).reshape(32, 8, 128)


def total_kernel(
    row_ref, selected_ref, parts_ref, lower_ref, panel_ref, mine_ref, other_ref
):
    scales = jnp.exp2(parts_ref[:, 24].astype(jnp.float32) * 0.125) * (1.0 / STEPS)
    core = lax.rem(row_ref[0], 2)
    for k in range(KS):
        rows = []
        for r in range(RB):
            keep = selected_ref[k, r * 16 + row_ref[0]].astype(jnp.float32)
            at = r * KS + k
            scale = scales[:, :, at : at + 1]
            halves = []
            for half in range(2):
                part = parts_ref[:, r * 6 + k * 2 + half].astype(jnp.float32)
                halves.append(jnp.sum(part * scale, axis=0))
            block = -(jnp.concatenate(halves, axis=1) * keep)
            panel_ref[k, r] = block
            rows.append(block)
        panel = jnp.concatenate(rows, axis=0)
        high = panel.astype(jnp.bfloat16)
        rest = panel - high.astype(jnp.float32)
        middle = rest.astype(jnp.bfloat16)
        low = (rest - middle.astype(jnp.float32)).astype(jnp.bfloat16)
        lower = lower_ref[k].astype(jnp.float32).reshape(RB * 8, W).astype(jnp.bfloat16)
        left = jnp.concatenate([lower, lower, lower], axis=0)
        right = jnp.concatenate([high, middle, low], axis=0)
        diag = lax.dot_general(
            left, right, (((0,), (0,)), ((), ())), preferred_element_type=jnp.float32
        )
        near, far = diag[:, :128], diag[:, 128:]
        mine_ref[:, k] = jnp.where(core == 0, near, far).reshape(32, 8, 128)
        other_ref[:, k] = jnp.where(core == 0, far, near).reshape(32, 8, 128)


def finish_kernel(sums_ref, diag_ref, out_ref):
    for k in range(KS):
        for half in range(2):
            at = slice(half * 128, (half + 1) * 128)
            out_ref[k, :, at] = diag_ref[k, :, at] - sums_ref[half, :, k].reshape(W, 128)


def call(kernel, name, shapes, scalars, arrays):
    vmem, smem = pl.BlockSpec(memory_space=pltpu.VMEM), pl.BlockSpec(memory_space=pltpu.SMEM)
    return pl.pallas_call(
        kernel,
        out_shape=shapes,
        in_specs=[smem] * len(scalars) + [vmem] * len(arrays),
        out_specs=jax.tree.map(lambda _: vmem, shapes),
        compiler_params=pltpu.CompilerParams(vmem_limit_bytes=LIMIT),
        name=name,
    )(*scalars, *arrays)


def per_device(inverse_tiles, lower_panels, diag_inverse, selected):
    row = lax.axis_index(ROW).astype(jnp.int32).reshape(1)
    lower = lower_panels[:, :, 0]
    shape = jax.ShapeDtypeStruct
    pieces = call(
        spread_kernel, "spread", shape((16, 2 * KS, 8, W), jnp.bfloat16), (row, selected), (lower,)
    )
    pieces = lax.all_to_all(pieces, ROW, 0, 0, tiled=True)
    pieces = pieces.reshape(16, 2, KS, 8, W).transpose(1, 0, 2, 3, 4).reshape(32, KS, 8, W)
    half = lax.all_to_all(pieces, COL, 0, 0, tiled=True)
    columns = lax.all_gather(half, "core", axis=0)
    tile = inverse_tiles.reshape(RB * W, 2 * W)
    parts = call(
        product_kernel, "product", shape((32, 25, 8, 128), jnp.int16), (), (tile, columns)
    )
    parts = lax.all_to_all(parts, COL, 0, 0, tiled=True)
    slab = shape((32, KS, 8, 128), jnp.float32)
    panel_out, mine, other = call(
        total_kernel,
        "total",
        (shape((KS, RB, 8, W), jnp.float32), slab, slab),
        (row, selected),
        (parts, lower),
    )
    mine = mine + lax.ppermute(other, "core", [(0, 1), (1, 0)])
    slices = lax.all_to_all(mine, PLANE, 0, 0, tiled=True)
    part = jnp.sum(slices, axis=0, keepdims=True)
    along = lax.all_to_all(jnp.broadcast_to(part, (8, KS, 8, 128)), LINE, 0, 0, tiled=True)
    whole = jnp.sum(along, axis=0, keepdims=True)
    back = lax.all_to_all(jnp.broadcast_to(whole, (32, KS, 8, 128)), PLANE, 0, 0, tiled=True)
    both = lax.all_gather(back, "core", axis=0)
    diagonal = call(
        finish_kernel, "finish", shape((KS, W, W), jnp.float32), (), (both, diag_inverse)
    )
    return (panel_out[:, :, None], diagonal)


def solution(mesh):
    finer = Mesh(mesh.devices.reshape(4, 2, 2, 8, 4), ROW + COL)
    in_specs = (
        P(None, ROW, None, None, COL, None),
        P(None, None, ROW, COL, None),
        P(),
        P(),
    )
    out_specs = (P(None, None, ROW, COL, None), P())
    return jax.shard_map(
        per_device, mesh=finer, in_specs=in_specs, out_specs=out_specs, check_vma=False
    )
```

```python
import jax
import jax.numpy as jnp
from jax import lax
from jax.experimental import pallas as pl
from jax.experimental.pallas import tpu as pltpu
from jax.sharding import Mesh, PartitionSpec as P

KS, RB, W = 3, 4, 256
ROW = ("x", "zh", "core")
COL = ("yh", "yl", "zl")
TARGET = ("yl", "zl", "yh")
PLANE = ("yh", "yl", "x")
LINE = ("zh", "zl")
STEPS = 32760.0
FLOOR = 1e-36
LIMIT = 24 * 1024 * 1024


def coded(block):
    peak = jnp.maximum(jnp.max(jnp.abs(block), axis=-1, keepdims=True), FLOOR)
    code = jnp.ceil(jnp.log2(peak) * 8.0 + 0.01)
    whole = jnp.round(block * (jnp.exp2(code * -0.125) * STEPS))
    return whole.astype(jnp.int32).astype(jnp.int16), code


def scale_of(codes):
    return jnp.exp2(codes.astype(jnp.float32) * 0.125) * (1.0 / STEPS)


def spread_kernel(row_ref, selected_ref, lower_ref, out_ref):
    for k in range(KS):
        for s in range(2):
            for h in range(2):
                r = 2 * s + h
                keep = selected_ref[k, r * 16 + row_ref[0]].astype(jnp.float32)
                block = (lower_ref[k, r].astype(jnp.float32) * keep).astype(jnp.bfloat16)
                for chip in range(8):
                    out_ref[chip * 2 + s, h * KS + k] = block


def product_kernel(tile_ref, cols_ref, out_ref):
    lane = lax.broadcasted_iota(jnp.int32, (W, 128), 1)
    codes = jnp.zeros((W, 128), jnp.float32)
    for k in range(KS):
        halves = []
        for s in range(2):
            part = cols_ref[s, :, k].reshape(16, 2, 8, W)
            halves += [part[:, y].reshape(W // 2, W) for y in range(2)]
        columns = jnp.concatenate(halves, axis=0)
        for r in range(RB):
            block = jnp.dot(
                tile_ref[r * W : (r + 1) * W, :], columns, preferred_element_type=jnp.float32
            )
            whole, code = coded(block)
            for half in range(2):
                out_ref[:, r * 6 + k * 2 + half] = whole[:, half * 128 : (half + 1) * 128].reshape(
                    32, 8, 128
                )
            codes = jnp.where(lane == r * KS + k, code, codes)
    out_ref[:, 24] = codes.astype(jnp.int32).astype(jnp.int16).reshape(32, 8, 128)


def total_kernel(
    row_ref, selected_ref, parts_ref, lower_ref, panel_ref, mine_ref, other_ref
):
    scales = scale_of(parts_ref[:, 24])
    core = lax.rem(row_ref[0], 2)
    for k in range(KS):
        rows = []
        for r in range(RB):
            keep = selected_ref[k, r * 16 + row_ref[0]].astype(jnp.float32)
            at = r * KS + k
            scale = scales[:, :, at : at + 1]
            halves = []
            for half in range(2):
                part = parts_ref[:, r * 6 + k * 2 + half].astype(jnp.float32)
                halves.append(jnp.sum(part * scale, axis=0))
            block = -(jnp.concatenate(halves, axis=1) * keep)
            panel_ref[k, r] = block
            rows.append(block)
        panel = jnp.concatenate(rows, axis=0)
        high = panel.astype(jnp.bfloat16)
        rest = panel - high.astype(jnp.float32)
        middle = rest.astype(jnp.bfloat16)
        low = (rest - middle.astype(jnp.float32)).astype(jnp.bfloat16)
        lower = lower_ref[k].astype(jnp.float32).reshape(RB * 8, W).astype(jnp.bfloat16)
        left = jnp.concatenate([lower, lower, lower], axis=0)
        right = jnp.concatenate([high, middle, low], axis=0)
        diag = lax.dot_general(
            left, right, (((0,), (0,)), ((), ())), preferred_element_type=jnp.float32
        )
        near, far = diag[:, :128], diag[:, 128:]
        mine_ref[:, k] = jnp.where(core == 0, near, far).reshape(32, 8, 128)
        other_ref[:, k] = jnp.where(core == 0, far, near).reshape(32, 8, 128)


def code_kernel(mine_ref, other_ref, out_ref):
    lane = lax.broadcasted_iota(jnp.int32, (32, 8, 128), 2)
    codes = jnp.zeros((32, 8, 128), jnp.float32)
    for k in range(KS):
        whole, code = coded(mine_ref[:, k] + other_ref[:, k])
        out_ref[:, k] = whole
        codes = jnp.where(lane == k, code, codes)
    out_ref[:, KS] = codes.astype(jnp.int32).astype(jnp.int16)


def plane_kernel(coded_ref, out_ref):
    scales = scale_of(coded_ref[:, KS])
    for k in range(KS):
        total = jnp.sum(coded_ref[:, k].astype(jnp.float32) * scales[:, :, k : k + 1], axis=0)
        for chip in range(8):
            out_ref[chip, k] = total


def line_kernel(sums_ref, out_ref):
    lane = lax.broadcasted_iota(jnp.int32, (8, 128), 1)
    codes = jnp.zeros((8, 128), jnp.float32)
    for k in range(KS):
        whole, code = coded(jnp.sum(sums_ref[:, k], axis=0))
        codes = jnp.where(lane == k, code, codes)
        for chip in range(32):
            out_ref[chip, k] = whole
    codes = codes.astype(jnp.int32).astype(jnp.int16)
    for chip in range(32):
        out_ref[chip, KS] = codes


def finish_kernel(coded_ref, diag_ref, out_ref):
    for half in range(2):
        at = slice(half * 128, (half + 1) * 128)
        scales = scale_of(coded_ref[half, :, KS])
        for k in range(KS):
            total = coded_ref[half, :, k].astype(jnp.float32) * scales[:, :, k : k + 1]
            out_ref[k, :, at] = diag_ref[k, :, at] - total.reshape(W, 128)


def call(kernel, name, shapes, scalars, arrays, limit=LIMIT):
    vmem, smem = pl.BlockSpec(memory_space=pltpu.VMEM), pl.BlockSpec(memory_space=pltpu.SMEM)
    return pl.pallas_call(
        kernel,
        out_shape=shapes,
        in_specs=[smem] * len(scalars) + [vmem] * len(arrays),
        out_specs=jax.tree.map(lambda _: vmem, shapes),
        compiler_params=pltpu.CompilerParams(vmem_limit_bytes=limit),
        name=name,
    )(*scalars, *arrays)


def per_device(inverse_tiles, lower_panels, diag_inverse, selected):
    row = lax.axis_index(ROW).astype(jnp.int32).reshape(1)
    lower = lower_panels[:, :, 0]
    shape = jax.ShapeDtypeStruct
    pieces = call(
        spread_kernel,
        "spread",
        shape((16, 2 * KS, 8, W), jnp.bfloat16),
        (row, selected),
        (lower,),
        limit=None,
    )
    pieces = lax.all_to_all(pieces, ROW, 0, 0, tiled=True).reshape(32, KS, 8, W)
    half = lax.all_to_all(pieces, TARGET, 0, 0, tiled=True)
    columns = lax.all_gather(half, "core", axis=0)
    tile = inverse_tiles.reshape(RB * W, 2 * W)
    parts = call(
        product_kernel, "product", shape((32, 25, 8, 128), jnp.int16), (), (tile, columns)
    )
    parts = lax.all_to_all(parts, COL, 0, 0, tiled=True)
    slab = shape((32, KS, 8, 128), jnp.float32)
    panel_out, mine, other = call(
        total_kernel,
        "total",
        (shape((KS, RB, 8, W), jnp.float32), slab, slab),
        (row, selected),
        (parts, lower),
    )
    other = lax.ppermute(other, "core", [(0, 1), (1, 0)])
    slices = call(code_kernel, "code", shape((32, 4, 8, 128), jnp.int16), (), (mine, other))
    slices = lax.all_to_all(slices, PLANE, 0, 0, tiled=True)
    along = call(plane_kernel, "plane", shape((8, KS, 8, 128), jnp.float32), (), (slices,))
    along = lax.all_to_all(along, LINE, 0, 0, tiled=True)
    whole = call(line_kernel, "line", shape((32, 4, 8, 128), jnp.int16), (), (along,))
    whole = lax.all_to_all(whole, PLANE, 0, 0, tiled=True)
    both = lax.all_gather(whole, "core", axis=0)
    diagonal = call(
        finish_kernel, "finish", shape((KS, W, W), jnp.float32), (), (both, diag_inverse)
    )
    return (panel_out[:, :, None], diagonal)


def solution(mesh):
    finer = Mesh(mesh.devices.reshape(4, 2, 2, 2, 4, 4), ROW + COL)
    in_specs = (
        P(None, ROW, None, None, COL, None),
        P(None, None, ROW, COL, None),
        P(),
        P(),
    )
    out_specs = (P(None, None, ROW, COL, None), P())
    return jax.shard_map(
        per_device, mesh=finer, in_specs=in_specs, out_specs=out_specs, check_vma=False
    )
```

```python
import jax
import jax.numpy as jnp
import numpy as np
from jax import lax
from jax.experimental import pallas as pl
from jax.experimental.pallas import tpu as pltpu
from jax.sharding import Mesh, PartitionSpec as P

KS, RB, W = 3, 4, 256
ROW = ("x", "zh", "core")
COL = ("yh", "yl", "zl")
TARGET = ("yl", "zl", "yh")
ALL = ROW + COL
STEPS = 32760.0
FLOOR = 1e-36
LIMIT = 24 * 1024 * 1024


def groups():
    index = np.arange(512).reshape(4, 2, 2, 8, 4)
    first, second = index[:, :, 0], index[:, :, 1]
    planes = [first.transpose(1, 3, 2, 0), second.transpose(2, 0, 1, 3)]
    lines = [first.transpose(0, 2, 1, 3), second.transpose(0, 1, 3, 2)]
    return [
        np.concatenate([part.reshape(-1, size) for part in parts]).tolist()
        for parts, size in ((planes, 32), (lines, 8))
    ]


def coded(block):
    peak = jnp.maximum(jnp.max(jnp.abs(block), axis=-1, keepdims=True), FLOOR)
    code = jnp.ceil(jnp.log2(peak) * 8.0 + 0.01)
    whole = jnp.round(block * (jnp.exp2(code * -0.125) * STEPS))
    return whole.astype(jnp.int32).astype(jnp.int16), code


def scale_of(codes):
    return jnp.exp2(codes.astype(jnp.float32) * 0.125) * (1.0 / STEPS)


def spread_kernel(row_ref, selected_ref, lower_ref, out_ref):
    for k in range(KS):
        for s in range(2):
            for h in range(2):
                r = 2 * s + h
                keep = selected_ref[k, r * 16 + row_ref[0]].astype(jnp.float32)
                block = (lower_ref[k, r].astype(jnp.float32) * keep).astype(jnp.bfloat16)
                for chip in range(8):
                    out_ref[chip * 2 + s, h * KS + k] = block


def product_kernel(tile_ref, cols_ref, out_ref):
    lane = lax.broadcasted_iota(jnp.int32, (W, 128), 1)
    codes = jnp.zeros((W, 128), jnp.float32)
    for k in range(KS):
        halves = []
        for s in range(2):
            part = cols_ref[s, :, k].reshape(16, 2, 8, W)
            halves += [part[:, y].reshape(W // 2, W) for y in range(2)]
        columns = jnp.concatenate(halves, axis=0)
        for r in range(RB):
            block = jnp.dot(
                tile_ref[r * W : (r + 1) * W, :], columns, preferred_element_type=jnp.float32
            )
            whole, code = coded(block)
            for half in range(2):
                out_ref[:, r * 6 + k * 2 + half] = whole[:, half * 128 : (half + 1) * 128].reshape(
                    32, 8, 128
                )
            codes = jnp.where(lane == r * KS + k, code, codes)
    out_ref[:, 24] = codes.astype(jnp.int32).astype(jnp.int16).reshape(32, 8, 128)


def total_kernel(
    row_ref, selected_ref, parts_ref, lower_ref, panel_ref, mine_ref, other_ref
):
    scales = scale_of(parts_ref[:, 24])
    core = lax.rem(row_ref[0], 2)
    for k in range(KS):
        rows = []
        for r in range(RB):
            keep = selected_ref[k, r * 16 + row_ref[0]].astype(jnp.float32)
            at = r * KS + k
            scale = scales[:, :, at : at + 1]
            halves = []
            for half in range(2):
                part = parts_ref[:, r * 6 + k * 2 + half].astype(jnp.float32)
                halves.append(jnp.sum(part * scale, axis=0))
            block = -(jnp.concatenate(halves, axis=1) * keep)
            panel_ref[k, r] = block
            rows.append(block)
        panel = jnp.concatenate(rows, axis=0)
        high = panel.astype(jnp.bfloat16)
        rest = panel - high.astype(jnp.float32)
        middle = rest.astype(jnp.bfloat16)
        low = (rest - middle.astype(jnp.float32)).astype(jnp.bfloat16)
        lower = lower_ref[k].astype(jnp.float32).reshape(RB * 8, W).astype(jnp.bfloat16)
        left = jnp.concatenate([lower, lower, lower], axis=0)
        right = jnp.concatenate([high, middle, low], axis=0)
        diag = lax.dot_general(
            left, right, (((0,), (0,)), ((), ())), preferred_element_type=jnp.float32
        )
        near, far = diag[:, :128], diag[:, 128:]
        mine_ref[:, k] = jnp.where(core == 0, near, far).reshape(32, 8, 128)
        other_ref[:, k] = jnp.where(core == 0, far, near).reshape(32, 8, 128)


def code_kernel(mine_ref, other_ref, out_ref):
    lane = lax.broadcasted_iota(jnp.int32, (32, 8, 128), 2)
    codes = jnp.zeros((32, 8, 128), jnp.float32)
    for k in range(KS):
        whole, code = coded(mine_ref[:, k] + other_ref[:, k])
        out_ref[:, k] = whole
        codes = jnp.where(lane == k, code, codes)
    out_ref[:, KS] = codes.astype(jnp.int32).astype(jnp.int16)


def plane_kernel(coded_ref, out_ref):
    scales = scale_of(coded_ref[:, KS])
    for k in range(KS):
        total = jnp.sum(coded_ref[:, k].astype(jnp.float32) * scales[:, :, k : k + 1], axis=0)
        for chip in range(8):
            out_ref[chip, k] = total


def line_kernel(sums_ref, out_ref):
    lane = lax.broadcasted_iota(jnp.int32, (8, 128), 1)
    codes = jnp.zeros((8, 128), jnp.float32)
    for k in range(KS):
        whole, code = coded(jnp.sum(sums_ref[:, k], axis=0))
        codes = jnp.where(lane == k, code, codes)
        for chip in range(32):
            out_ref[chip, k] = whole
    codes = codes.astype(jnp.int32).astype(jnp.int16)
    for chip in range(32):
        out_ref[chip, KS] = codes


def finish_kernel(coded_ref, diag_ref, out_ref):
    for half in range(2):
        at = slice(half * 128, (half + 1) * 128)
        scales = scale_of(coded_ref[half, :, KS])
        for k in range(KS):
            total = coded_ref[half, :, k].astype(jnp.float32) * scales[:, :, k : k + 1]
            out_ref[k, :, at] = diag_ref[k, :, at] - total.reshape(W, 128)


def call(kernel, name, shapes, scalars, arrays, limit=LIMIT):
    vmem, smem = pl.BlockSpec(memory_space=pltpu.VMEM), pl.BlockSpec(memory_space=pltpu.SMEM)
    return pl.pallas_call(
        kernel,
        out_shape=shapes,
        in_specs=[smem] * len(scalars) + [vmem] * len(arrays),
        out_specs=jax.tree.map(lambda _: vmem, shapes),
        compiler_params=pltpu.CompilerParams(vmem_limit_bytes=limit),
        name=name,
    )(*scalars, *arrays)


def per_device(inverse_tiles, lower_panels, diag_inverse, selected):
    row = lax.axis_index(ROW).astype(jnp.int32).reshape(1)
    lower = lower_panels[:, :, 0]
    shape = jax.ShapeDtypeStruct
    pieces = call(
        spread_kernel,
        "spread",
        shape((16, 2 * KS, 8, W), jnp.bfloat16),
        (row, selected),
        (lower,),
        limit=None,
    )
    pieces = lax.all_to_all(pieces, ROW, 0, 0, tiled=True).reshape(32, KS, 8, W)
    half = lax.all_to_all(pieces, TARGET, 0, 0, tiled=True)
    columns = lax.all_gather(half, "core", axis=0)
    tile = inverse_tiles.reshape(RB * W, 2 * W)
    parts = call(
        product_kernel, "product", shape((32, 25, 8, 128), jnp.int16), (), (tile, columns)
    )
    parts = lax.all_to_all(parts, COL, 0, 0, tiled=True)
    slab = shape((32, KS, 8, 128), jnp.float32)
    panel_out, mine, other = call(
        total_kernel,
        "total",
        (shape((KS, RB, 8, W), jnp.float32), slab, slab),
        (row, selected),
        (parts, lower),
    )
    plane, line = groups()
    other = lax.ppermute(other, "core", [(0, 1), (1, 0)])
    slices = call(code_kernel, "code", shape((32, 4, 8, 128), jnp.int16), (), (mine, other))
    slices = lax.all_to_all(slices, ALL, 0, 0, axis_index_groups=plane, tiled=True)
    along = call(plane_kernel, "plane", shape((8, KS, 8, 128), jnp.float32), (), (slices,))
    along = lax.all_to_all(along, ALL, 0, 0, axis_index_groups=line, tiled=True)
    whole = call(line_kernel, "line", shape((32, 4, 8, 128), jnp.int16), (), (along,))
    whole = lax.all_to_all(whole, ALL, 0, 0, axis_index_groups=plane, tiled=True)
    both = lax.all_gather(whole, "core", axis=0)
    diagonal = call(
        finish_kernel, "finish", shape((KS, W, W), jnp.float32), (), (both, diag_inverse)
    )
    return (panel_out[:, :, None], diagonal)


def solution(mesh):
    finer = Mesh(mesh.devices.reshape(4, 2, 2, 2, 4, 4), ROW + COL)
    in_specs = (
        P(None, ROW, None, None, COL, None),
        P(None, None, ROW, COL, None),
        P(),
        P(),
    )
    out_specs = (P(None, None, ROW, COL, None), P())
    return jax.shard_map(
        per_device, mesh=finer, in_specs=in_specs, out_specs=out_specs, check_vma=False
    )
```

```python
import jax
import jax.numpy as jnp
import numpy as np
from jax import lax
from jax.experimental import pallas as pl
from jax.experimental.pallas import tpu as pltpu
from jax.sharding import Mesh, PartitionSpec as P

KS, RB, W = 3, 4, 256
ROW = ("x", "zh", "core")
COL = ("yh", "yl", "zl")
TARGET = ("yl", "zl", "yh")
ALL = ROW + COL
STEPS = 32760.0
FLOOR = 1e-36
LIMIT = 24 * 1024 * 1024


def groups():
    index = np.arange(512).reshape(4, 2, 2, 8, 4)
    first, second = index[:, :, 1], index[:, :, 0]
    planes = [first.transpose(1, 3, 2, 0), second.transpose(2, 0, 1, 3)]
    lines = [first.transpose(0, 2, 1, 3), second.transpose(0, 1, 3, 2)]
    return [
        np.concatenate([part.reshape(-1, size) for part in parts]).tolist()
        for parts, size in ((planes, 32), (lines, 8))
    ]


def coded(block):
    peak = jnp.maximum(jnp.max(jnp.abs(block), axis=-1, keepdims=True), FLOOR)
    code = jnp.ceil(jnp.log2(peak) * 8.0 + 0.01)
    whole = jnp.round(block * (jnp.exp2(code * -0.125) * STEPS))
    return whole.astype(jnp.int32).astype(jnp.int16), code


def scale_of(codes):
    return jnp.exp2(codes.astype(jnp.float32) * 0.125) * (1.0 / STEPS)


def spread_kernel(row_ref, selected_ref, lower_ref, out_ref):
    for k in range(KS):
        for s in range(2):
            for h in range(2):
                r = 2 * s + h
                keep = selected_ref[k, r * 16 + row_ref[0]].astype(jnp.float32)
                block = (lower_ref[k, r].astype(jnp.float32) * keep).astype(jnp.bfloat16)
                for chip in range(8):
                    out_ref[chip * 2 + s, h * KS + k] = block


def product_kernel(tile_ref, cols_ref, out_ref):
    lane = lax.broadcasted_iota(jnp.int32, (W, 128), 1)
    codes = jnp.zeros((W, 128), jnp.float32)
    for k in range(KS):
        halves = []
        for s in range(2):
            part = cols_ref[s, :, k].reshape(16, 2, 8, W)
            halves += [part[:, y].reshape(W // 2, W) for y in range(2)]
        columns = jnp.concatenate(halves, axis=0)
        for r in range(RB):
            block = jnp.dot(
                tile_ref[r * W : (r + 1) * W, :], columns, preferred_element_type=jnp.float32
            )
            whole, code = coded(block)
            for half in range(2):
                out_ref[:, r * 6 + k * 2 + half] = whole[:, half * 128 : (half + 1) * 128].reshape(
                    32, 8, 128
                )
            codes = jnp.where(lane == r * KS + k, code, codes)
    out_ref[:, 24] = codes.astype(jnp.int32).astype(jnp.int16).reshape(32, 8, 128)


def total_kernel(
    row_ref, selected_ref, parts_ref, lower_ref, panel_ref, mine_ref, other_ref
):
    scales = scale_of(parts_ref[:, 24])
    core = lax.rem(row_ref[0], 2)
    for k in range(KS):
        rows = []
        for r in range(RB):
            keep = selected_ref[k, r * 16 + row_ref[0]].astype(jnp.float32)
            at = r * KS + k
            scale = scales[:, :, at : at + 1]
            halves = []
            for half in range(2):
                part = parts_ref[:, r * 6 + k * 2 + half].astype(jnp.float32)
                halves.append(jnp.sum(part * scale, axis=0))
            block = -(jnp.concatenate(halves, axis=1) * keep)
            panel_ref[k, r] = block
            rows.append(block)
        panel = jnp.concatenate(rows, axis=0)
        high = panel.astype(jnp.bfloat16)
        rest = panel - high.astype(jnp.float32)
        middle = rest.astype(jnp.bfloat16)
        low = (rest - middle.astype(jnp.float32)).astype(jnp.bfloat16)
        lower = lower_ref[k].astype(jnp.float32).reshape(RB * 8, W).astype(jnp.bfloat16)
        left = jnp.concatenate([lower, lower, lower], axis=0)
        right = jnp.concatenate([high, middle, low], axis=0)
        diag = lax.dot_general(
            left, right, (((0,), (0,)), ((), ())), preferred_element_type=jnp.float32
        )
        near, far = diag[:, :128], diag[:, 128:]
        mine_ref[:, k] = jnp.where(core == 0, near, far).reshape(32, 8, 128)
        other_ref[:, k] = jnp.where(core == 0, far, near).reshape(32, 8, 128)


def code_kernel(mine_ref, other_ref, out_ref):
    lane = lax.broadcasted_iota(jnp.int32, (32, 8, 128), 2)
    codes = jnp.zeros((32, 8, 128), jnp.float32)
    for k in range(KS):
        whole, code = coded(mine_ref[:, k] + other_ref[:, k])
        out_ref[:, k] = whole
        codes = jnp.where(lane == k, code, codes)
    out_ref[:, KS] = codes.astype(jnp.int32).astype(jnp.int16)


def plane_kernel(coded_ref, out_ref):
    scales = scale_of(coded_ref[:, KS])
    for k in range(KS):
        total = jnp.sum(coded_ref[:, k].astype(jnp.float32) * scales[:, :, k : k + 1], axis=0)
        for chip in range(8):
            out_ref[chip, k] = total


def line_kernel(sums_ref, out_ref):
    lane = lax.broadcasted_iota(jnp.int32, (8, 128), 1)
    codes = jnp.zeros((8, 128), jnp.float32)
    for k in range(KS):
        whole, code = coded(jnp.sum(sums_ref[:, k], axis=0))
        codes = jnp.where(lane == k, code, codes)
        for chip in range(32):
            out_ref[chip, k] = whole
    codes = codes.astype(jnp.int32).astype(jnp.int16)
    for chip in range(32):
        out_ref[chip, KS] = codes


def finish_kernel(coded_ref, diag_ref, out_ref):
    for half in range(2):
        at = slice(half * 128, (half + 1) * 128)
        scales = scale_of(coded_ref[half, :, KS])
        for k in range(KS):
            total = coded_ref[half, :, k].astype(jnp.float32) * scales[:, :, k : k + 1]
            out_ref[k, :, at] = diag_ref[k, :, at] - total.reshape(W, 128)


def call(kernel, name, shapes, scalars, arrays, limit=LIMIT):
    vmem, smem = pl.BlockSpec(memory_space=pltpu.VMEM), pl.BlockSpec(memory_space=pltpu.SMEM)
    return pl.pallas_call(
        kernel,
        out_shape=shapes,
        in_specs=[smem] * len(scalars) + [vmem] * len(arrays),
        out_specs=jax.tree.map(lambda _: vmem, shapes),
        compiler_params=pltpu.CompilerParams(vmem_limit_bytes=limit),
        name=name,
    )(*scalars, *arrays)


def per_device(inverse_tiles, lower_panels, diag_inverse, selected):
    row = lax.axis_index(ROW).astype(jnp.int32).reshape(1)
    lower = lower_panels[:, :, 0]
    shape = jax.ShapeDtypeStruct
    pieces = call(
        spread_kernel,
        "spread",
        shape((16, 2 * KS, 8, W), jnp.bfloat16),
        (row, selected),
        (lower,),
        limit=None,
    )
    pieces = lax.all_to_all(pieces, ROW, 0, 0, tiled=True).reshape(32, KS, 8, W)
    half = lax.all_to_all(pieces, TARGET, 0, 0, tiled=True)
    columns = lax.all_gather(half, "core", axis=0)
    tile = inverse_tiles.reshape(RB * W, 2 * W)
    parts = call(
        product_kernel, "product", shape((32, 25, 8, 128), jnp.int16), (), (tile, columns)
    )
    parts = lax.all_to_all(parts, COL, 0, 0, tiled=True)
    slab = shape((32, KS, 8, 128), jnp.float32)
    panel_out, mine, other = call(
        total_kernel,
        "total",
        (shape((KS, RB, 8, W), jnp.float32), slab, slab),
        (row, selected),
        (parts, lower),
    )
    plane, line = groups()
    other = lax.ppermute(other, "core", [(0, 1), (1, 0)])
    slices = call(code_kernel, "code", shape((32, 4, 8, 128), jnp.int16), (), (mine, other))
    slices = lax.all_to_all(slices, ALL, 0, 0, axis_index_groups=plane, tiled=True)
    along = call(plane_kernel, "plane", shape((8, KS, 8, 128), jnp.float32), (), (slices,))
    along = lax.all_to_all(along, ALL, 0, 0, axis_index_groups=line, tiled=True)
    whole = call(line_kernel, "line", shape((32, 4, 8, 128), jnp.int16), (), (along,))
    whole = lax.all_to_all(whole, ALL, 0, 0, axis_index_groups=plane, tiled=True)
    both = lax.all_gather(whole, "core", axis=0)
    diagonal = call(
        finish_kernel, "finish", shape((KS, W, W), jnp.float32), (), (both, diag_inverse)
    )
    return (panel_out[:, :, None], diagonal)


def solution(mesh):
    finer = Mesh(mesh.devices.reshape(4, 2, 2, 2, 4, 4), ROW + COL)
    in_specs = (
        P(None, ROW, None, None, COL, None),
        P(None, None, ROW, COL, None),
        P(),
        P(),
    )
    out_specs = (P(None, None, ROW, COL, None), P())
    return jax.shard_map(
        per_device, mesh=finer, in_specs=in_specs, out_specs=out_specs, check_vma=False
    )
```

```python
import functools

import jax
import jax.numpy as jnp
import numpy as np
from jax import lax
from jax.experimental import pallas as pl
from jax.experimental.pallas import tpu as pltpu
from jax.sharding import Mesh, PartitionSpec as P

KS, RB, W = 3, 4, 256
ROW = ("x", "zh", "core")
COL = ("yh", "yl", "zl")
TARGET = ("yl", "zl", "yh")
ALL = ROW + COL
STEPS = 32760.0
FLOOR = 1e-36
LIMIT = 24 * 1024 * 1024


def grouped(size, *parts):
    return np.concatenate([part.reshape(-1, size) for part in parts]).tolist()


def groups():
    index = np.arange(512).reshape(4, 2, 2, 8, 4)
    first, second = index[:, :, 0], index[:, :, 1]
    split = first.reshape(4, 2, 2, 4, 4)
    near = grouped(4, split.transpose(0, 1, 2, 4, 3), second)
    far = grouped(8, split.transpose(0, 1, 3, 2, 4), second.transpose(0, 1, 3, 2))
    plane = grouped(32, first.transpose(2, 0, 1, 3), second.transpose(1, 3, 2, 0))
    line = grouped(8, first.transpose(0, 1, 3, 2), second.transpose(0, 2, 1, 3))
    return near, far, plane, line


def coded(block):
    peak = jnp.maximum(jnp.max(jnp.abs(block), axis=-1, keepdims=True), FLOOR)
    code = jnp.ceil(jnp.log2(peak) * 8.0 + 0.01)
    whole = jnp.round(block * (jnp.exp2(code * -0.125) * STEPS))
    return whole.astype(jnp.int32).astype(jnp.int16), code


def scale_of(codes):
    return jnp.exp2(codes.astype(jnp.float32) * 0.125) * (1.0 / STEPS)


def spread_kernel(row_ref, selected_ref, lower_ref, out_ref):
    for k in range(KS):
        for s in range(2):
            for h in range(2):
                r = 2 * s + h
                keep = selected_ref[k, r * 16 + row_ref[0]].astype(jnp.float32)
                block = (lower_ref[k, r].astype(jnp.float32) * keep).astype(jnp.bfloat16)
                for chip in range(8):
                    out_ref[chip * 2 + s, h * KS + k] = block


def by_peer(block, core):
    if core == 0:
        return block.reshape(2, 4, 4, 8, 128).transpose(1, 0, 2, 3, 4).reshape(32, 8, 128)
    return block.reshape(8, 4, 8, 128).transpose(1, 0, 2, 3).reshape(32, 8, 128)


def product_kernel(row_ref, tile_ref, cols_ref, out_ref):
    def body(core):
        lane = lax.broadcasted_iota(jnp.int32, (W, 128), 1)
        codes = jnp.zeros((W, 128), jnp.float32)
        for k in range(KS):
            halves = []
            for s in range(2):
                part = cols_ref[s, :, k].reshape(16, 2, 8, W)
                halves += [part[:, y].reshape(W // 2, W) for y in range(2)]
            columns = jnp.concatenate(halves, axis=0)
            for r in range(RB):
                block = jnp.dot(
                    tile_ref[r * W : (r + 1) * W, :], columns, preferred_element_type=jnp.float32
                )
                whole, code = coded(block)
                for half in range(2):
                    out_ref[:, r * 6 + k * 2 + half] = by_peer(
                        whole[:, half * 128 : (half + 1) * 128], core
                    )
                codes = jnp.where(lane == r * KS + k, code, codes)
        out_ref[:, 24] = by_peer(codes.astype(jnp.int32).astype(jnp.int16), core)

    for core in range(2):
        pl.when(lax.rem(row_ref[0], 2) == core)(functools.partial(body, core))


def fold_kernel(parts_ref, out_ref):
    scales = scale_of(parts_ref[:, 24])
    lane = lax.broadcasted_iota(jnp.int32, (8, 8, 128), 2)
    codes = jnp.zeros((8, 8, 128), jnp.float32)
    for k in range(KS):
        for r in range(RB):
            at = r * KS + k
            halves = []
            for half in range(2):
                part = parts_ref[:, r * 6 + k * 2 + half].astype(jnp.float32)
                part = part * scales[:, :, at : at + 1]
                halves.append(jnp.sum(part.reshape(4, 8, 8, 128), axis=0))
            whole, code = coded(jnp.concatenate(halves, axis=2))
            for half in range(2):
                out_ref[:, r * 6 + k * 2 + half] = whole[:, :, half * 128 : (half + 1) * 128]
            codes = jnp.where(lane == at, code, codes)
    out_ref[:, 24] = codes.astype(jnp.int32).astype(jnp.int16)


def total_kernel(
    row_ref, selected_ref, parts_ref, lower_ref, panel_ref, mine_ref, other_ref
):
    scales = scale_of(parts_ref[:, 24])
    core = lax.rem(row_ref[0], 2)
    for k in range(KS):
        rows = []
        for r in range(RB):
            keep = selected_ref[k, r * 16 + row_ref[0]].astype(jnp.float32)
            at = r * KS + k
            scale = scales[:, :, at : at + 1]
            halves = []
            for half in range(2):
                part = parts_ref[:, r * 6 + k * 2 + half].astype(jnp.float32)
                halves.append(jnp.sum(part * scale, axis=0))
            block = -(jnp.concatenate(halves, axis=1) * keep)
            panel_ref[k, r] = block
            rows.append(block)
        panel = jnp.concatenate(rows, axis=0)
        high = panel.astype(jnp.bfloat16)
        rest = panel - high.astype(jnp.float32)
        middle = rest.astype(jnp.bfloat16)
        low = (rest - middle.astype(jnp.float32)).astype(jnp.bfloat16)
        lower = lower_ref[k].astype(jnp.float32).reshape(RB * 8, W).astype(jnp.bfloat16)
        left = jnp.concatenate([lower, lower, lower], axis=0)
        right = jnp.concatenate([high, middle, low], axis=0)
        diag = lax.dot_general(
            left, right, (((0,), (0,)), ((), ())), preferred_element_type=jnp.float32
        )
        near, far = diag[:, :128], diag[:, 128:]
        mine_ref[:, k] = jnp.where(core == 0, near, far).reshape(32, 8, 128)
        other_ref[:, k] = jnp.where(core == 0, far, near).reshape(32, 8, 128)


def code_kernel(mine_ref, other_ref, out_ref):
    lane = lax.broadcasted_iota(jnp.int32, (32, 8, 128), 2)
    codes = jnp.zeros((32, 8, 128), jnp.float32)
    for k in range(KS):
        whole, code = coded(mine_ref[:, k] + other_ref[:, k])
        out_ref[:, k] = whole
        codes = jnp.where(lane == k, code, codes)
    out_ref[:, KS] = codes.astype(jnp.int32).astype(jnp.int16)


def plane_kernel(coded_ref, out_ref):
    scales = scale_of(coded_ref[:, KS])
    for k in range(KS):
        total = jnp.sum(coded_ref[:, k].astype(jnp.float32) * scales[:, :, k : k + 1], axis=0)
        for chip in range(8):
            out_ref[chip, k] = total


def line_kernel(sums_ref, out_ref):
    lane = lax.broadcasted_iota(jnp.int32, (8, 128), 1)
    codes = jnp.zeros((8, 128), jnp.float32)
    for k in range(KS):
        whole, code = coded(jnp.sum(sums_ref[:, k], axis=0))
        codes = jnp.where(lane == k, code, codes)
        for chip in range(32):
            out_ref[chip, k] = whole
    codes = codes.astype(jnp.int32).astype(jnp.int16)
    for chip in range(32):
        out_ref[chip, KS] = codes


def finish_kernel(coded_ref, diag_ref, out_ref):
    for half in range(2):
        at = slice(half * 128, (half + 1) * 128)
        scales = scale_of(coded_ref[half, :, KS])
        for k in range(KS):
            total = coded_ref[half, :, k].astype(jnp.float32) * scales[:, :, k : k + 1]
            out_ref[k, :, at] = diag_ref[k, :, at] - total.reshape(W, 128)


def call(kernel, name, shapes, scalars, arrays, limit=LIMIT):
    vmem, smem = pl.BlockSpec(memory_space=pltpu.VMEM), pl.BlockSpec(memory_space=pltpu.SMEM)
    return pl.pallas_call(
        kernel,
        out_shape=shapes,
        in_specs=[smem] * len(scalars) + [vmem] * len(arrays),
        out_specs=jax.tree.map(lambda _: vmem, shapes),
        compiler_params=pltpu.CompilerParams(vmem_limit_bytes=limit),
        name=name,
    )(*scalars, *arrays)


def per_device(inverse_tiles, lower_panels, diag_inverse, selected):
    row = lax.axis_index(ROW).astype(jnp.int32).reshape(1)
    near, far, plane, line = groups()
    lower = lower_panels[:, :, 0]
    shape = jax.ShapeDtypeStruct
    pieces = call(
        spread_kernel,
        "spread",
        shape((16, 2 * KS, 8, W), jnp.bfloat16),
        (row, selected),
        (lower,),
        limit=None,
    )
    pieces = lax.all_to_all(pieces, ROW, 0, 0, tiled=True).reshape(32, KS, 8, W)
    half = lax.all_to_all(pieces, TARGET, 0, 0, tiled=True)
    columns = lax.all_gather(half, "core", axis=0)
    tile = inverse_tiles.reshape(RB * W, 2 * W)
    parts = call(
        product_kernel, "product", shape((32, 25, 8, 128), jnp.int16), (row,), (tile, columns)
    )
    parts = lax.all_to_all(parts, ALL, 0, 0, axis_index_groups=near, tiled=True)
    parts = call(fold_kernel, "fold", shape((8, 25, 8, 128), jnp.int16), (), (parts,))
    parts = lax.all_to_all(parts, ALL, 0, 0, axis_index_groups=far, tiled=True)
    slab = shape((32, KS, 8, 128), jnp.float32)
    panel_out, mine, other = call(
        total_kernel,
        "total",
        (shape((KS, RB, 8, W), jnp.float32), slab, slab),
        (row, selected),
        (parts, lower),
    )
    other = lax.ppermute(other, "core", [(0, 1), (1, 0)])
    slices = call(code_kernel, "code", shape((32, 4, 8, 128), jnp.int16), (), (mine, other))
    slices = lax.all_to_all(slices, ALL, 0, 0, axis_index_groups=plane, tiled=True)
    along = call(plane_kernel, "plane", shape((8, KS, 8, 128), jnp.float32), (), (slices,))
    along = lax.all_to_all(along, ALL, 0, 0, axis_index_groups=line, tiled=True)
    whole = call(line_kernel, "line", shape((32, 4, 8, 128), jnp.int16), (), (along,))
    whole = lax.all_to_all(whole, ALL, 0, 0, axis_index_groups=plane, tiled=True)
    both = lax.all_gather(whole, "core", axis=0)
    diagonal = call(
        finish_kernel, "finish", shape((KS, W, W), jnp.float32), (), (both, diag_inverse)
    )
    return (panel_out[:, :, None], diagonal)


def solution(mesh):
    finer = Mesh(mesh.devices.reshape(4, 2, 2, 2, 4, 4), ROW + COL)
    in_specs = (
        P(None, ROW, None, None, COL, None),
        P(None, None, ROW, COL, None),
        P(),
        P(),
    )
    out_specs = (P(None, None, ROW, COL, None), P())
    return jax.shard_map(
        per_device, mesh=finer, in_specs=in_specs, out_specs=out_specs, check_vma=False
    )
```

```python
import functools

import jax
import jax.numpy as jnp
import numpy as np
from jax import lax
from jax.experimental import pallas as pl
from jax.experimental.pallas import tpu as pltpu
from jax.sharding import Mesh, PartitionSpec as P

KS, RB, W = 3, 4, 256
ROW = ("x", "zh", "core")
COL = ("yh", "yl", "zl")
TARGET = ("yl", "zl", "yh")
ALL = ROW + COL
STEPS = 32760.0
FLOOR = 1e-36
LIMIT = 24 * 1024 * 1024


def grouped(size, *parts):
    return np.concatenate([part.reshape(-1, size) for part in parts]).tolist()


def groups():
    index = np.arange(512).reshape(4, 2, 2, 8, 4)
    first, second = index[:, :, 0], index[:, :, 1]
    split = second.reshape(4, 2, 2, 4, 4)
    near = grouped(4, first, split.transpose(0, 1, 2, 4, 3))
    far = grouped(8, first.transpose(0, 1, 3, 2), split.transpose(0, 1, 3, 2, 4))
    plane = grouped(32, first.transpose(2, 0, 1, 3), second.transpose(1, 3, 2, 0))
    line = grouped(8, first.transpose(0, 1, 3, 2), second.transpose(0, 2, 1, 3))
    return near, far, plane, line


def coded(block):
    peak = jnp.maximum(jnp.max(jnp.abs(block), axis=-1, keepdims=True), FLOOR)
    code = jnp.ceil(jnp.log2(peak) * 8.0 + 0.01)
    whole = jnp.round(block * (jnp.exp2(code * -0.125) * STEPS))
    return whole.astype(jnp.int32).astype(jnp.int16), code


def scale_of(codes):
    return jnp.exp2(codes.astype(jnp.float32) * 0.125) * (1.0 / STEPS)


def spread_kernel(row_ref, selected_ref, lower_ref, out_ref):
    for k in range(KS):
        for s in range(2):
            for h in range(2):
                r = 2 * s + h
                keep = selected_ref[k, r * 16 + row_ref[0]].astype(jnp.float32)
                block = (lower_ref[k, r].astype(jnp.float32) * keep).astype(jnp.bfloat16)
                for chip in range(8):
                    out_ref[chip * 2 + s, h * KS + k] = block


def by_peer(block, core):
    if core == 1:
        return block.reshape(2, 4, 4, 8, 128).transpose(1, 0, 2, 3, 4).reshape(32, 8, 128)
    return block.reshape(8, 4, 8, 128).transpose(1, 0, 2, 3).reshape(32, 8, 128)


def product_kernel(row_ref, tile_ref, cols_ref, out_ref):
    def body(core):
        lane = lax.broadcasted_iota(jnp.int32, (W, 128), 1)
        codes = jnp.zeros((W, 128), jnp.float32)
        for k in range(KS):
            halves = []
            for s in range(2):
                part = cols_ref[s, :, k].reshape(16, 2, 8, W)
                halves += [part[:, y].reshape(W // 2, W) for y in range(2)]
            columns = jnp.concatenate(halves, axis=0)
            for r in range(RB):
                block = jnp.dot(
                    tile_ref[r * W : (r + 1) * W, :], columns, preferred_element_type=jnp.float32
                )
                whole, code = coded(block)
                for half in range(2):
                    out_ref[:, r * 6 + k * 2 + half] = by_peer(
                        whole[:, half * 128 : (half + 1) * 128], core
                    )
                codes = jnp.where(lane == r * KS + k, code, codes)
        out_ref[:, 24] = by_peer(codes.astype(jnp.int32).astype(jnp.int16), core)

    for core in range(2):
        pl.when(lax.rem(row_ref[0], 2) == core)(functools.partial(body, core))


def fold_kernel(parts_ref, out_ref):
    scales = scale_of(parts_ref[:, 24])
    lane = lax.broadcasted_iota(jnp.int32, (8, 8, 128), 2)
    codes = jnp.zeros((8, 8, 128), jnp.float32)
    for k in range(KS):
        for r in range(RB):
            at = r * KS + k
            halves = []
            for half in range(2):
                part = parts_ref[:, r * 6 + k * 2 + half].astype(jnp.float32)
                part = part * scales[:, :, at : at + 1]
                halves.append(jnp.sum(part.reshape(4, 8, 8, 128), axis=0))
            whole, code = coded(jnp.concatenate(halves, axis=2))
            for half in range(2):
                out_ref[:, r * 6 + k * 2 + half] = whole[:, :, half * 128 : (half + 1) * 128]
            codes = jnp.where(lane == at, code, codes)
    out_ref[:, 24] = codes.astype(jnp.int32).astype(jnp.int16)


def total_kernel(row_ref, selected_ref, parts_ref, panel_ref, mine_ref, other_ref):
    scales = scale_of(parts_ref[:, 24])
    core = lax.rem(row_ref[0], 2)
    for k in range(KS):
        for r in range(RB):
            keep = selected_ref[k, r * 16 + row_ref[0]].astype(jnp.float32)
            at = r * KS + k
            scale = scales[:, :, at : at + 1]
            halves = []
            for half in range(2):
                part = parts_ref[:, r * 6 + k * 2 + half].astype(jnp.float32)
                halves.append(-(jnp.sum(part * scale, axis=0) * keep))
            panel_ref[k, r] = jnp.concatenate(halves, axis=1)
            mine_ref[k, r] = jnp.where(core == 0, halves[0], halves[1])
            other_ref[k, r] = jnp.where(core == 0, halves[1], halves[0])


def diag_kernel(mine_ref, theirs_ref, lower_ref, pair_ref, out_ref):
    lane = lax.broadcasted_iota(jnp.int32, (32, 8, 128), 2)
    codes = jnp.zeros((32, 8, 128), jnp.float32)
    for k in range(KS):
        rows = [ref[k].reshape(RB * 8, 128) for ref in (mine_ref, theirs_ref)]
        rows = jnp.concatenate(rows, axis=0)
        high = rows.astype(jnp.bfloat16)
        rest = rows - high.astype(jnp.float32)
        middle = rest.astype(jnp.bfloat16)
        low = (rest - middle.astype(jnp.float32)).astype(jnp.bfloat16)
        lower = [
            ref[k].astype(jnp.float32).reshape(RB * 8, W).astype(jnp.bfloat16)
            for ref in (lower_ref, pair_ref)
        ]
        diag = lax.dot_general(
            jnp.concatenate(lower * 3, axis=0),
            jnp.concatenate([high, middle, low], axis=0),
            (((0,), (0,)), ((), ())),
            preferred_element_type=jnp.float32,
        )
        whole, code = coded(diag.reshape(32, 8, 128))
        out_ref[:, k] = whole
        codes = jnp.where(lane == k, code, codes)
    out_ref[:, KS] = codes.astype(jnp.int32).astype(jnp.int16)


def plane_kernel(coded_ref, out_ref):
    scales = scale_of(coded_ref[:, KS])
    for k in range(KS):
        total = jnp.sum(coded_ref[:, k].astype(jnp.float32) * scales[:, :, k : k + 1], axis=0)
        for chip in range(8):
            out_ref[chip, k] = total


def line_kernel(sums_ref, out_ref):
    lane = lax.broadcasted_iota(jnp.int32, (8, 128), 1)
    codes = jnp.zeros((8, 128), jnp.float32)
    for k in range(KS):
        whole, code = coded(jnp.sum(sums_ref[:, k], axis=0))
        codes = jnp.where(lane == k, code, codes)
        for chip in range(32):
            out_ref[chip, k] = whole
    codes = codes.astype(jnp.int32).astype(jnp.int16)
    for chip in range(32):
        out_ref[chip, KS] = codes


def finish_kernel(coded_ref, diag_ref, out_ref):
    for half in range(2):
        at = slice(half * 128, (half + 1) * 128)
        scales = scale_of(coded_ref[half, :, KS])
        for k in range(KS):
            total = coded_ref[half, :, k].astype(jnp.float32) * scales[:, :, k : k + 1]
            out_ref[k, :, at] = diag_ref[k, :, at] - total.reshape(W, 128)


def call(kernel, name, shapes, scalars, arrays, limit=LIMIT):
    vmem, smem = pl.BlockSpec(memory_space=pltpu.VMEM), pl.BlockSpec(memory_space=pltpu.SMEM)
    return pl.pallas_call(
        kernel,
        out_shape=shapes,
        in_specs=[smem] * len(scalars) + [vmem] * len(arrays),
        out_specs=jax.tree.map(lambda _: vmem, shapes),
        compiler_params=pltpu.CompilerParams(vmem_limit_bytes=limit),
        name=name,
    )(*scalars, *arrays)


def per_device(inverse_tiles, lower_panels, diag_inverse, selected):
    row = lax.axis_index(ROW).astype(jnp.int32).reshape(1)
    near, far, plane, line = groups()
    lower = lower_panels[:, :, 0]
    shape = jax.ShapeDtypeStruct
    pieces = call(
        spread_kernel,
        "spread",
        shape((16, 2 * KS, 8, W), jnp.bfloat16),
        (row, selected),
        (lower,),
        limit=None,
    )
    pieces = lax.all_to_all(pieces, ROW, 0, 0, tiled=True).reshape(32, KS, 8, W)
    half = lax.all_to_all(pieces, TARGET, 0, 0, tiled=True)
    columns = lax.all_gather(half, "core", axis=0)
    late, columns = lax.optimization_barrier((lower, columns))
    with jax.named_scope("pair"):
        pair = lax.ppermute(late, "core", [(0, 1), (1, 0)])
    tile = inverse_tiles.reshape(RB * W, 2 * W)
    parts = call(
        product_kernel, "product", shape((32, 25, 8, 128), jnp.int16), (row,), (tile, columns)
    )
    parts = lax.all_to_all(parts, ALL, 0, 0, axis_index_groups=near, tiled=True)
    parts = call(fold_kernel, "fold", shape((8, 25, 8, 128), jnp.int16), (), (parts,))
    parts = lax.all_to_all(parts, ALL, 0, 0, axis_index_groups=far, tiled=True)
    columns_half = shape((KS, RB, 8, 128), jnp.float32)
    panel_out, mine, other = call(
        total_kernel,
        "total",
        (shape((KS, RB, 8, W), jnp.float32), columns_half, columns_half),
        (row, selected),
        (parts,),
    )
    theirs = lax.ppermute(other, "core", [(0, 1), (1, 0)])
    slices = call(
        diag_kernel,
        "diag",
        shape((32, 4, 8, 128), jnp.int16),
        (),
        (mine, theirs, lower, pair),
    )
    slices = lax.all_to_all(slices, ALL, 0, 0, axis_index_groups=plane, tiled=True)
    along = call(plane_kernel, "plane", shape((8, KS, 8, 128), jnp.float32), (), (slices,))
    along = lax.all_to_all(along, ALL, 0, 0, axis_index_groups=line, tiled=True)
    whole = call(line_kernel, "line", shape((32, 4, 8, 128), jnp.int16), (), (along,))
    whole = lax.all_to_all(whole, ALL, 0, 0, axis_index_groups=plane, tiled=True)
    both = lax.all_gather(whole, "core", axis=0)
    diagonal = call(
        finish_kernel, "finish", shape((KS, W, W), jnp.float32), (), (both, diag_inverse)
    )
    return (panel_out[:, :, None], diagonal)


def solution(mesh):
    finer = Mesh(mesh.devices.reshape(4, 2, 2, 2, 4, 4), ROW + COL)
    in_specs = (
        P(None, ROW, None, None, COL, None),
        P(None, None, ROW, COL, None),
        P(),
        P(),
    )
    out_specs = (P(None, None, ROW, COL, None), P())
    return jax.shard_map(
        per_device, mesh=finer, in_specs=in_specs, out_specs=out_specs, check_vma=False
    )
```

```python
import functools

import jax
import jax.numpy as jnp
import numpy as np
from jax import lax
from jax.experimental import pallas as pl
from jax.experimental.pallas import tpu as pltpu
from jax.sharding import Mesh, PartitionSpec as P

KS, RB, W = 3, 4, 256
ROW = ("x", "zh", "core")
COL = ("yh", "yl", "zl")
TARGET = ("yl", "zl", "yh")
ALL = ROW + COL
STEPS = 32760.0
FLOOR = 1e-36
LIMIT = 24 * 1024 * 1024


def grouped(size, *parts):
    return np.concatenate([part.reshape(-1, size) for part in parts]).tolist()


def groups():
    index = np.arange(512).reshape(4, 2, 2, 8, 4)
    first, second = index[:, :, 0], index[:, :, 1]
    split = second.reshape(4, 2, 2, 4, 4)
    near = grouped(4, first, split.transpose(0, 1, 2, 4, 3))
    far = grouped(8, first.transpose(0, 1, 3, 2), split.transpose(0, 1, 3, 2, 4))
    plane = grouped(32, first.transpose(2, 0, 1, 3), second.transpose(1, 3, 2, 0))
    line = grouped(8, first.transpose(0, 1, 3, 2), second.transpose(0, 2, 1, 3))
    return near, far, plane, line


def coded(block):
    peak = jnp.maximum(jnp.max(jnp.abs(block), axis=-1, keepdims=True), FLOOR)
    code = jnp.ceil(jnp.log2(peak) * 8.0 + 0.01)
    whole = jnp.round(block * (jnp.exp2(code * -0.125) * STEPS))
    return whole.astype(jnp.int32).astype(jnp.int16), code


def scale_of(codes):
    return jnp.exp2(codes.astype(jnp.float32) * 0.125) * (1.0 / STEPS)


def spread_kernel(row_ref, selected_ref, lower_ref, out_ref):
    for k in range(KS):
        for s in range(2):
            for h in range(2):
                r = 2 * s + h
                keep = selected_ref[k, r * 16 + row_ref[0]].astype(jnp.float32)
                block = (lower_ref[k, r].astype(jnp.float32) * keep).astype(jnp.bfloat16)
                for chip in range(8):
                    out_ref[chip * 2 + s, h * KS + k] = block


def by_peer(block, core):
    if core == 1:
        return block.reshape(2, 4, 4, 8, 128).transpose(1, 0, 2, 3, 4).reshape(32, 8, 128)
    return block.reshape(8, 4, 8, 128).transpose(1, 0, 2, 3).reshape(32, 8, 128)


def product_kernel(row_ref, pair_ref, tile_ref, cols_ref, out_ref):
    del pair_ref

    def body(core):
        lane = lax.broadcasted_iota(jnp.int32, (W, 128), 1)
        codes = jnp.zeros((W, 128), jnp.float32)
        for k in range(KS):
            halves = []
            for s in range(2):
                part = cols_ref[s, :, k].reshape(16, 2, 8, W)
                halves += [part[:, y].reshape(W // 2, W) for y in range(2)]
            columns = jnp.concatenate(halves, axis=0)
            for r in range(RB):
                block = jnp.dot(
                    tile_ref[r * W : (r + 1) * W, :], columns, preferred_element_type=jnp.float32
                )
                whole, code = coded(block)
                for half in range(2):
                    out_ref[:, r * 6 + k * 2 + half] = by_peer(
                        whole[:, half * 128 : (half + 1) * 128], core
                    )
                codes = jnp.where(lane == r * KS + k, code, codes)
        out_ref[:, 24] = by_peer(codes.astype(jnp.int32).astype(jnp.int16), core)

    for core in range(2):
        pl.when(lax.rem(row_ref[0], 2) == core)(functools.partial(body, core))


def fold_kernel(parts_ref, out_ref):
    scales = scale_of(parts_ref[:, 24])
    lane = lax.broadcasted_iota(jnp.int32, (8, 8, 128), 2)
    codes = jnp.zeros((8, 8, 128), jnp.float32)
    for k in range(KS):
        for r in range(RB):
            at = r * KS + k
            halves = []
            for half in range(2):
                part = parts_ref[:, r * 6 + k * 2 + half].astype(jnp.float32)
                part = part * scales[:, :, at : at + 1]
                halves.append(jnp.sum(part.reshape(4, 8, 8, 128), axis=0))
            whole, code = coded(jnp.concatenate(halves, axis=2))
            for half in range(2):
                out_ref[:, r * 6 + k * 2 + half] = whole[:, :, half * 128 : (half + 1) * 128]
            codes = jnp.where(lane == at, code, codes)
    out_ref[:, 24] = codes.astype(jnp.int32).astype(jnp.int16)


def total_kernel(row_ref, selected_ref, parts_ref, panel_ref, mine_ref, other_ref):
    scales = scale_of(parts_ref[:, 24])
    core = lax.rem(row_ref[0], 2)
    for k in range(KS):
        for r in range(RB):
            keep = selected_ref[k, r * 16 + row_ref[0]].astype(jnp.float32)
            at = r * KS + k
            scale = scales[:, :, at : at + 1]
            halves = []
            for half in range(2):
                part = parts_ref[:, r * 6 + k * 2 + half].astype(jnp.float32)
                halves.append(-(jnp.sum(part * scale, axis=0) * keep))
            panel_ref[k, r] = jnp.concatenate(halves, axis=1)
            mine_ref[k, r] = jnp.where(core == 0, halves[0], halves[1])
            other_ref[k, r] = jnp.where(core == 0, halves[1], halves[0])


def diag_kernel(mine_ref, theirs_ref, lower_ref, pair_ref, out_ref):
    lane = lax.broadcasted_iota(jnp.int32, (32, 8, 128), 2)
    codes = jnp.zeros((32, 8, 128), jnp.float32)
    for k in range(KS):
        rows = [ref[k].reshape(RB * 8, 128) for ref in (mine_ref, theirs_ref)]
        rows = jnp.concatenate(rows, axis=0)
        high = rows.astype(jnp.bfloat16)
        rest = rows - high.astype(jnp.float32)
        middle = rest.astype(jnp.bfloat16)
        low = (rest - middle.astype(jnp.float32)).astype(jnp.bfloat16)
        lower = [
            ref[k].astype(jnp.float32).reshape(RB * 8, W).astype(jnp.bfloat16)
            for ref in (lower_ref, pair_ref)
        ]
        diag = lax.dot_general(
            jnp.concatenate(lower * 3, axis=0),
            jnp.concatenate([high, middle, low], axis=0),
            (((0,), (0,)), ((), ())),
            preferred_element_type=jnp.float32,
        )
        whole, code = coded(diag.reshape(32, 8, 128))
        out_ref[:, k] = whole
        codes = jnp.where(lane == k, code, codes)
    out_ref[:, KS] = codes.astype(jnp.int32).astype(jnp.int16)


def plane_kernel(coded_ref, out_ref):
    scales = scale_of(coded_ref[:, KS])
    for k in range(KS):
        total = jnp.sum(coded_ref[:, k].astype(jnp.float32) * scales[:, :, k : k + 1], axis=0)
        for chip in range(8):
            out_ref[chip, k] = total


def line_kernel(sums_ref, out_ref):
    lane = lax.broadcasted_iota(jnp.int32, (8, 128), 1)
    codes = jnp.zeros((8, 128), jnp.float32)
    for k in range(KS):
        whole, code = coded(jnp.sum(sums_ref[:, k], axis=0))
        codes = jnp.where(lane == k, code, codes)
        for chip in range(32):
            out_ref[chip, k] = whole
    codes = codes.astype(jnp.int32).astype(jnp.int16)
    for chip in range(32):
        out_ref[chip, KS] = codes


def finish_kernel(coded_ref, diag_ref, out_ref):
    for half in range(2):
        at = slice(half * 128, (half + 1) * 128)
        scales = scale_of(coded_ref[half, :, KS])
        for k in range(KS):
            total = coded_ref[half, :, k].astype(jnp.float32) * scales[:, :, k : k + 1]
            out_ref[k, :, at] = diag_ref[k, :, at] - total.reshape(W, 128)


def call(kernel, name, shapes, scalars, arrays, limit=LIMIT, early=()):
    vmem, smem = pl.BlockSpec(memory_space=pltpu.VMEM), pl.BlockSpec(memory_space=pltpu.SMEM)
    return pl.pallas_call(
        kernel,
        out_shape=shapes,
        in_specs=[smem] * len(scalars)
        + [pl.BlockSpec(memory_space=pl.ANY)] * len(early)
        + [vmem] * len(arrays),
        out_specs=jax.tree.map(lambda _: vmem, shapes),
        compiler_params=pltpu.CompilerParams(vmem_limit_bytes=limit),
        name=name,
    )(*scalars, *early, *arrays)


def per_device(inverse_tiles, lower_panels, diag_inverse, selected):
    row = lax.axis_index(ROW).astype(jnp.int32).reshape(1)
    near, far, plane, line = groups()
    lower = lower_panels[:, :, 0]
    shape = jax.ShapeDtypeStruct
    pieces = call(
        spread_kernel,
        "spread",
        shape((16, 2 * KS, 8, W), jnp.bfloat16),
        (row, selected),
        (lower,),
        limit=None,
    )
    pieces = lax.all_to_all(pieces, ROW, 0, 0, tiled=True).reshape(32, KS, 8, W)
    pair = lax.ppermute(lower, "core", [(0, 1), (1, 0)])
    half = lax.all_to_all(pieces, TARGET, 0, 0, tiled=True)
    columns = lax.all_gather(half, "core", axis=0)
    tile = inverse_tiles.reshape(RB * W, 2 * W)
    parts = call(
        product_kernel, "product", shape((32, 25, 8, 128), jnp.int16), (row,), (tile, columns), early=(pair,)
    )
    parts = lax.all_to_all(parts, ALL, 0, 0, axis_index_groups=near, tiled=True)
    parts = call(fold_kernel, "fold", shape((8, 25, 8, 128), jnp.int16), (), (parts,))
    parts = lax.all_to_all(parts, ALL, 0, 0, axis_index_groups=far, tiled=True)
    columns_half = shape((KS, RB, 8, 128), jnp.float32)
    panel_out, mine, other = call(
        total_kernel,
        "total",
        (shape((KS, RB, 8, W), jnp.float32), columns_half, columns_half),
        (row, selected),
        (parts,),
    )
    theirs = lax.ppermute(other, "core", [(0, 1), (1, 0)])
    slices = call(
        diag_kernel,
        "diag",
        shape((32, 4, 8, 128), jnp.int16),
        (),
        (mine, theirs, lower, pair),
    )
    slices = lax.all_to_all(slices, ALL, 0, 0, axis_index_groups=plane, tiled=True)
    along = call(plane_kernel, "plane", shape((8, KS, 8, 128), jnp.float32), (), (slices,))
    along = lax.all_to_all(along, ALL, 0, 0, axis_index_groups=line, tiled=True)
    whole = call(line_kernel, "line", shape((32, 4, 8, 128), jnp.int16), (), (along,))
    whole = lax.all_to_all(whole, ALL, 0, 0, axis_index_groups=plane, tiled=True)
    both = lax.all_gather(whole, "core", axis=0)
    diagonal = call(
        finish_kernel, "finish", shape((KS, W, W), jnp.float32), (), (both, diag_inverse)
    )
    return (panel_out[:, :, None], diagonal)


def solution(mesh):
    finer = Mesh(mesh.devices.reshape(4, 2, 2, 2, 4, 4), ROW + COL)
    in_specs = (
        P(None, ROW, None, None, COL, None),
        P(None, None, ROW, COL, None),
        P(),
        P(),
    )
    out_specs = (P(None, None, ROW, COL, None), P())
    return jax.shard_map(
        per_device, mesh=finer, in_specs=in_specs, out_specs=out_specs, check_vma=False
    )
```

```python
import functools

import jax
import jax.numpy as jnp
import numpy as np
from jax import lax
from jax.experimental import pallas as pl
from jax.experimental.pallas import tpu as pltpu
from jax.sharding import Mesh, PartitionSpec as P

KS, RB, W = 3, 4, 256
ROW = ("x", "zh", "core")
COL = ("yh", "yl", "zl")
TARGET = ("yl", "zl", "yh")
ALL = ROW + COL
STEPS = 32760.0
FLOOR = 1e-36
LIMIT = 24 * 1024 * 1024


def grouped(size, *parts):
    return np.concatenate([part.reshape(-1, size) for part in parts]).tolist()


def groups():
    index = np.arange(512).reshape(4, 2, 2, 8, 4)
    first, second = index[:, :, 0], index[:, :, 1]
    split = second.reshape(4, 2, 4, 2, 4)
    near = grouped(4, first, split.transpose(0, 1, 3, 4, 2))
    far = grouped(8, first.transpose(0, 1, 3, 2), split)
    plane = grouped(32, first.transpose(2, 0, 1, 3), second.transpose(1, 3, 2, 0))
    line = grouped(8, first.transpose(0, 1, 3, 2), second.transpose(0, 2, 1, 3))
    return near, far, plane, line


def coded(block):
    peak = jnp.maximum(jnp.max(jnp.abs(block), axis=-1, keepdims=True), FLOOR)
    code = jnp.ceil(jnp.log2(peak) * 8.0 + 0.01)
    whole = jnp.round(block * (jnp.exp2(code * -0.125) * STEPS))
    return whole.astype(jnp.int32).astype(jnp.int16), code


def scale_of(codes):
    return jnp.exp2(codes.astype(jnp.float32) * 0.125) * (1.0 / STEPS)


def spread_kernel(row_ref, selected_ref, lower_ref, out_ref):
    for k in range(KS):
        for s in range(2):
            for h in range(2):
                r = 2 * s + h
                keep = selected_ref[k, r * 16 + row_ref[0]].astype(jnp.float32)
                block = (lower_ref[k, r].astype(jnp.float32) * keep).astype(jnp.bfloat16)
                for chip in range(8):
                    out_ref[chip * 2 + s, h * KS + k] = block


def by_peer(block, core):
    if core == 1:
        return block.reshape(32, 8, 128)
    return block.reshape(8, 4, 8, 128).transpose(1, 0, 2, 3).reshape(32, 8, 128)


def product_kernel(row_ref, pair_ref, tile_ref, cols_ref, out_ref):
    del pair_ref

    def body(core):
        lane = lax.broadcasted_iota(jnp.int32, (W, 128), 1)
        codes = jnp.zeros((W, 128), jnp.float32)
        for k in range(KS):
            halves = []
            for s in range(2):
                part = cols_ref[s, :, k].reshape(16, 2, 8, W)
                halves += [part[:, y].reshape(W // 2, W) for y in range(2)]
            columns = jnp.concatenate(halves, axis=0)
            for r in range(RB):
                block = jnp.dot(
                    tile_ref[r * W : (r + 1) * W, :], columns, preferred_element_type=jnp.float32
                )
                whole, code = coded(block)
                for half in range(2):
                    out_ref[:, r * 6 + k * 2 + half] = by_peer(
                        whole[:, half * 128 : (half + 1) * 128], core
                    )
                codes = jnp.where(lane == r * KS + k, code, codes)
        out_ref[:, 24] = by_peer(codes.astype(jnp.int32).astype(jnp.int16), core)

    for core in range(2):
        pl.when(lax.rem(row_ref[0], 2) == core)(functools.partial(body, core))


def fold_kernel(parts_ref, out_ref):
    scales = scale_of(parts_ref[:, 24])
    lane = lax.broadcasted_iota(jnp.int32, (8, 8, 128), 2)
    codes = jnp.zeros((8, 8, 128), jnp.float32)
    for k in range(KS):
        for r in range(RB):
            at = r * KS + k
            halves = []
            for half in range(2):
                part = parts_ref[:, r * 6 + k * 2 + half].astype(jnp.float32)
                part = part * scales[:, :, at : at + 1]
                halves.append(jnp.sum(part.reshape(4, 8, 8, 128), axis=0))
            whole, code = coded(jnp.concatenate(halves, axis=2))
            for half in range(2):
                out_ref[:, r * 6 + k * 2 + half] = whole[:, :, half * 128 : (half + 1) * 128]
            codes = jnp.where(lane == at, code, codes)
    out_ref[:, 24] = codes.astype(jnp.int32).astype(jnp.int16)


def total_kernel(row_ref, selected_ref, parts_ref, panel_ref, mine_ref, other_ref):
    scales = scale_of(parts_ref[:, 24])
    core = lax.rem(row_ref[0], 2)
    for k in range(KS):
        for r in range(RB):
            keep = selected_ref[k, r * 16 + row_ref[0]].astype(jnp.float32)
            at = r * KS + k
            scale = scales[:, :, at : at + 1]
            halves = []
            for half in range(2):
                part = parts_ref[:, r * 6 + k * 2 + half].astype(jnp.float32)
                halves.append(-(jnp.sum(part * scale, axis=0) * keep))
            panel_ref[k, r] = jnp.concatenate(halves, axis=1)
            mine_ref[k, r] = jnp.where(core == 0, halves[0], halves[1])
            other_ref[k, r] = jnp.where(core == 0, halves[1], halves[0])


def diag_kernel(mine_ref, theirs_ref, lower_ref, pair_ref, out_ref):
    lane = lax.broadcasted_iota(jnp.int32, (32, 8, 128), 2)
    codes = jnp.zeros((32, 8, 128), jnp.float32)
    for k in range(KS):
        rows = [ref[k].reshape(RB * 8, 128) for ref in (mine_ref, theirs_ref)]
        rows = jnp.concatenate(rows, axis=0)
        high = rows.astype(jnp.bfloat16)
        rest = rows - high.astype(jnp.float32)
        middle = rest.astype(jnp.bfloat16)
        low = (rest - middle.astype(jnp.float32)).astype(jnp.bfloat16)
        lower = [
            ref[k].astype(jnp.float32).reshape(RB * 8, W).astype(jnp.bfloat16)
            for ref in (lower_ref, pair_ref)
        ]
        diag = lax.dot_general(
            jnp.concatenate(lower * 3, axis=0),
            jnp.concatenate([high, middle, low], axis=0),
            (((0,), (0,)), ((), ())),
            preferred_element_type=jnp.float32,
        )
        whole, code = coded(diag.reshape(32, 8, 128))
        out_ref[:, k] = whole
        codes = jnp.where(lane == k, code, codes)
    out_ref[:, KS] = codes.astype(jnp.int32).astype(jnp.int16)


def plane_kernel(coded_ref, out_ref):
    scales = scale_of(coded_ref[:, KS])
    for k in range(KS):
        total = jnp.sum(coded_ref[:, k].astype(jnp.float32) * scales[:, :, k : k + 1], axis=0)
        for chip in range(8):
            out_ref[chip, k] = total


def line_kernel(sums_ref, out_ref):
    lane = lax.broadcasted_iota(jnp.int32, (8, 128), 1)
    codes = jnp.zeros((8, 128), jnp.float32)
    for k in range(KS):
        whole, code = coded(jnp.sum(sums_ref[:, k], axis=0))
        codes = jnp.where(lane == k, code, codes)
        for chip in range(32):
            out_ref[chip, k] = whole
    codes = codes.astype(jnp.int32).astype(jnp.int16)
    for chip in range(32):
        out_ref[chip, KS] = codes


def finish_kernel(coded_ref, diag_ref, out_ref):
    for half in range(2):
        at = slice(half * 128, (half + 1) * 128)
        scales = scale_of(coded_ref[half, :, KS])
        for k in range(KS):
            total = coded_ref[half, :, k].astype(jnp.float32) * scales[:, :, k : k + 1]
            out_ref[k, :, at] = diag_ref[k, :, at] - total.reshape(W, 128)


def call(kernel, name, shapes, scalars, arrays, limit=LIMIT, early=()):
    vmem, smem = pl.BlockSpec(memory_space=pltpu.VMEM), pl.BlockSpec(memory_space=pltpu.SMEM)
    return pl.pallas_call(
        kernel,
        out_shape=shapes,
        in_specs=[smem] * len(scalars)
        + [pl.BlockSpec(memory_space=pl.ANY)] * len(early)
        + [vmem] * len(arrays),
        out_specs=jax.tree.map(lambda _: vmem, shapes),
        compiler_params=pltpu.CompilerParams(vmem_limit_bytes=limit),
        name=name,
    )(*scalars, *early, *arrays)


def per_device(inverse_tiles, lower_panels, diag_inverse, selected):
    row = lax.axis_index(ROW).astype(jnp.int32).reshape(1)
    near, far, plane, line = groups()
    lower = lower_panels[:, :, 0]
    shape = jax.ShapeDtypeStruct
    pieces = call(
        spread_kernel,
        "spread",
        shape((16, 2 * KS, 8, W), jnp.bfloat16),
        (row, selected),
        (lower,),
        limit=None,
    )
    pieces = lax.all_to_all(pieces, ROW, 0, 0, tiled=True).reshape(32, KS, 8, W)
    pair = lax.ppermute(lower, "core", [(0, 1), (1, 0)])
    half = lax.all_to_all(pieces, TARGET, 0, 0, tiled=True)
    columns = lax.all_gather(half, "core", axis=0)
    tile = inverse_tiles.reshape(RB * W, 2 * W)
    parts = call(
        product_kernel, "product", shape((32, 25, 8, 128), jnp.int16), (row,), (tile, columns), early=(pair,)
    )
    parts = lax.all_to_all(parts, ALL, 0, 0, axis_index_groups=near, tiled=True)
    parts = call(fold_kernel, "fold", shape((8, 25, 8, 128), jnp.int16), (), (parts,))
    parts = lax.all_to_all(parts, ALL, 0, 0, axis_index_groups=far, tiled=True)
    columns_half = shape((KS, RB, 8, 128), jnp.float32)
    panel_out, mine, other = call(
        total_kernel,
        "total",
        (shape((KS, RB, 8, W), jnp.float32), columns_half, columns_half),
        (row, selected),
        (parts,),
    )
    theirs = lax.ppermute(other, "core", [(0, 1), (1, 0)])
    slices = call(
        diag_kernel,
        "diag",
        shape((32, 4, 8, 128), jnp.int16),
        (),
        (mine, theirs, lower, pair),
    )
    slices = lax.all_to_all(slices, ALL, 0, 0, axis_index_groups=plane, tiled=True)
    along = call(plane_kernel, "plane", shape((8, KS, 8, 128), jnp.float32), (), (slices,))
    along = lax.all_to_all(along, ALL, 0, 0, axis_index_groups=line, tiled=True)
    whole = call(line_kernel, "line", shape((32, 4, 8, 128), jnp.int16), (), (along,))
    whole = lax.all_to_all(whole, ALL, 0, 0, axis_index_groups=plane, tiled=True)
    both = lax.all_gather(whole, "core", axis=0)
    diagonal = call(
        finish_kernel, "finish", shape((KS, W, W), jnp.float32), (), (both, diag_inverse)
    )
    return (panel_out[:, :, None], diagonal)


def solution(mesh):
    finer = Mesh(mesh.devices.reshape(4, 2, 2, 2, 4, 4), ROW + COL)
    in_specs = (
        P(None, ROW, None, None, COL, None),
        P(None, None, ROW, COL, None),
        P(),
        P(),
    )
    out_specs = (P(None, None, ROW, COL, None), P())
    return jax.shard_map(
        per_device, mesh=finer, in_specs=in_specs, out_specs=out_specs, check_vma=False
    )
```

```python
import functools

import jax
import jax.numpy as jnp
import numpy as np
from jax import lax
from jax.experimental import pallas as pl
from jax.experimental.pallas import tpu as pltpu
from jax.sharding import Mesh, PartitionSpec as P

KS, RB, W = 3, 4, 256
ROW = ("x", "zh", "core")
COL = ("yh", "yl", "zl")
TARGET = ("yl", "zl", "yh")
ALL = ROW + COL
STEPS = 32760.0
FLOOR = 1e-36
LIMIT = 24 * 1024 * 1024


def grouped(size, *parts):
    return np.concatenate([part.reshape(-1, size) for part in parts]).tolist()


def groups():
    index = np.arange(512).reshape(4, 2, 2, 8, 4)
    first, second = index[:, :, 0], index[:, :, 1]
    split = second.reshape(4, 2, 4, 2, 4)
    near = grouped(4, first, split.transpose(0, 1, 3, 4, 2))
    far = grouped(8, first.transpose(0, 1, 3, 2), split)
    plane = grouped(32, first.transpose(2, 0, 1, 3), second.transpose(1, 3, 2, 0))
    line = grouped(8, first.transpose(0, 1, 3, 2), second.transpose(0, 2, 1, 3))
    return near, far, plane, line


def coded(block):
    peak = jnp.maximum(jnp.max(jnp.abs(block), axis=-1, keepdims=True), FLOOR)
    code = jnp.ceil(jnp.log2(peak) * 8.0 + 0.01)
    whole = jnp.round(block * (jnp.exp2(code * -0.125) * STEPS))
    return whole.astype(jnp.int32).astype(jnp.int16), code


def scale_of(codes):
    return jnp.exp2(codes.astype(jnp.float32) * 0.125) * (1.0 / STEPS)


def spread_kernel(row_ref, selected_ref, lower_ref, out_ref):
    for k in range(KS):
        for s in range(2):
            for h in range(2):
                r = 2 * s + h
                keep = selected_ref[k, r * 16 + row_ref[0]].astype(jnp.float32)
                block = (lower_ref[k, r].astype(jnp.float32) * keep).astype(jnp.bfloat16)
                for chip in range(8):
                    out_ref[chip * 2 + s, h * KS + k] = block


def by_peer(block, core):
    if core == 1:
        return block.reshape(32, 8, 128)
    return block.reshape(8, 4, 8, 128).transpose(1, 0, 2, 3).reshape(32, 8, 128)


def product_kernel(row_ref, pair_ref, tile_ref, cols_ref, out_ref):
    del pair_ref

    def body(core):
        lane = lax.broadcasted_iota(jnp.int32, (W, 128), 1)
        codes = jnp.zeros((W, 128), jnp.float32)
        for k in range(KS):
            halves = []
            for s in range(2):
                part = cols_ref[s, :, k].reshape(16, 2, 8, W)
                halves += [part[:, y].reshape(W // 2, W) for y in range(2)]
            columns = jnp.concatenate(halves, axis=0)
            for r in range(RB):
                block = jnp.dot(
                    tile_ref[r * W : (r + 1) * W, :], columns, preferred_element_type=jnp.float32
                )
                whole, code = coded(block)
                for half in range(2):
                    out_ref[:, r * 6 + k * 2 + half] = by_peer(
                        whole[:, half * 128 : (half + 1) * 128], core
                    )
                codes = jnp.where(lane == r * KS + k, code, codes)
        out_ref[:, 24] = by_peer(codes.astype(jnp.int32).astype(jnp.int16), core)

    for core in range(2):
        pl.when(lax.rem(row_ref[0], 2) == core)(functools.partial(body, core))


def fold_kernel(parts_ref, out_ref):
    scales = scale_of(parts_ref[:, 24])
    lane = lax.broadcasted_iota(jnp.int32, (8, 8, 128), 2)
    codes = jnp.zeros((8, 8, 128), jnp.float32)
    for k in range(KS):
        for r in range(RB):
            at = r * KS + k
            halves = []
            for half in range(2):
                part = parts_ref[:, r * 6 + k * 2 + half].astype(jnp.float32)
                part = part * scales[:, :, at : at + 1]
                halves.append(jnp.sum(part.reshape(4, 8, 8, 128), axis=0))
            whole, code = coded(jnp.concatenate(halves, axis=2))
            for half in range(2):
                out_ref[:, r * 6 + k * 2 + half] = whole[:, :, half * 128 : (half + 1) * 128]
            codes = jnp.where(lane == at, code, codes)
    out_ref[:, 24] = codes.astype(jnp.int32).astype(jnp.int16)


def total_kernel(row_ref, selected_ref, parts_ref, panel_ref, mine_ref, other_ref):
    scales = scale_of(parts_ref[:, 24])
    core = lax.rem(row_ref[0], 2)
    for k in range(KS):
        for r in range(RB):
            keep = selected_ref[k, r * 16 + row_ref[0]].astype(jnp.float32)
            at = r * KS + k
            scale = scales[:, :, at : at + 1]
            halves = []
            for half in range(2):
                part = parts_ref[:, r * 6 + k * 2 + half].astype(jnp.float32)
                halves.append(-(jnp.sum(part * scale, axis=0) * keep))
            panel_ref[k, r] = jnp.concatenate(halves, axis=1)
            mine_ref[k, r] = jnp.where(core == 0, halves[0], halves[1])
            other_ref[k, r] = jnp.where(core == 0, halves[1], halves[0])


def diag_kernel(row_ref, mine_ref, both_ref, lower_ref, pair_ref, out_ref):
    partner = 1 - lax.rem(row_ref[0], 2)
    lane = lax.broadcasted_iota(jnp.int32, (32, 8, 128), 2)
    codes = jnp.zeros((32, 8, 128), jnp.float32)
    for k in range(KS):
        rows = [part.reshape(RB * 8, 128) for part in (mine_ref[k], both_ref[partner, k])]
        rows = jnp.concatenate(rows, axis=0)
        high = rows.astype(jnp.bfloat16)
        rest = rows - high.astype(jnp.float32)
        middle = rest.astype(jnp.bfloat16)
        low = (rest - middle.astype(jnp.float32)).astype(jnp.bfloat16)
        lower = [
            ref[k].astype(jnp.float32).reshape(RB * 8, W).astype(jnp.bfloat16)
            for ref in (lower_ref, pair_ref)
        ]
        diag = lax.dot_general(
            jnp.concatenate(lower * 3, axis=0),
            jnp.concatenate([high, middle, low], axis=0),
            (((0,), (0,)), ((), ())),
            preferred_element_type=jnp.float32,
        )
        whole, code = coded(diag.reshape(32, 8, 128))
        out_ref[:, k] = whole
        codes = jnp.where(lane == k, code, codes)
    out_ref[:, KS] = codes.astype(jnp.int32).astype(jnp.int16)


def plane_kernel(coded_ref, out_ref):
    scales = scale_of(coded_ref[:, KS])
    for k in range(KS):
        total = jnp.sum(coded_ref[:, k].astype(jnp.float32) * scales[:, :, k : k + 1], axis=0)
        for chip in range(8):
            out_ref[chip, k] = total


def line_kernel(sums_ref, out_ref):
    lane = lax.broadcasted_iota(jnp.int32, (8, 128), 1)
    codes = jnp.zeros((8, 128), jnp.float32)
    for k in range(KS):
        whole, code = coded(jnp.sum(sums_ref[:, k], axis=0))
        codes = jnp.where(lane == k, code, codes)
        for chip in range(32):
            out_ref[chip, k] = whole
    codes = codes.astype(jnp.int32).astype(jnp.int16)
    for chip in range(32):
        out_ref[chip, KS] = codes


def finish_kernel(coded_ref, diag_ref, out_ref):
    for half in range(2):
        at = slice(half * 128, (half + 1) * 128)
        scales = scale_of(coded_ref[half, :, KS])
        for k in range(KS):
            total = coded_ref[half, :, k].astype(jnp.float32) * scales[:, :, k : k + 1]
            out_ref[k, :, at] = diag_ref[k, :, at] - total.reshape(W, 128)


def call(kernel, name, shapes, scalars, arrays, limit=LIMIT, early=()):
    vmem, smem = pl.BlockSpec(memory_space=pltpu.VMEM), pl.BlockSpec(memory_space=pltpu.SMEM)
    return pl.pallas_call(
        kernel,
        out_shape=shapes,
        in_specs=[smem] * len(scalars)
        + [pl.BlockSpec(memory_space=pl.ANY)] * len(early)
        + [vmem] * len(arrays),
        out_specs=jax.tree.map(lambda _: vmem, shapes),
        compiler_params=pltpu.CompilerParams(vmem_limit_bytes=limit),
        name=name,
    )(*scalars, *early, *arrays)


def per_device(inverse_tiles, lower_panels, diag_inverse, selected):
    row = lax.axis_index(ROW).astype(jnp.int32).reshape(1)
    near, far, plane, line = groups()
    lower = lower_panels[:, :, 0]
    shape = jax.ShapeDtypeStruct
    pieces = call(
        spread_kernel,
        "spread",
        shape((16, 2 * KS, 8, W), jnp.bfloat16),
        (row, selected),
        (lower,),
        limit=None,
    )
    pieces = lax.all_to_all(pieces, ROW, 0, 0, tiled=True).reshape(32, KS, 8, W)
    pair = lax.ppermute(lower, "core", [(0, 1), (1, 0)])
    half = lax.all_to_all(pieces, TARGET, 0, 0, tiled=True)
    columns = lax.all_gather(half, "core", axis=0)
    tile = inverse_tiles.reshape(RB * W, 2 * W)
    parts = call(
        product_kernel, "product", shape((32, 25, 8, 128), jnp.int16), (row,), (tile, columns), early=(pair,)
    )
    parts = lax.all_to_all(parts, ALL, 0, 0, axis_index_groups=near, tiled=True)
    parts = call(fold_kernel, "fold", shape((8, 25, 8, 128), jnp.int16), (), (parts,))
    parts = lax.all_to_all(parts, ALL, 0, 0, axis_index_groups=far, tiled=True)
    columns_half = shape((KS, RB, 8, 128), jnp.float32)
    panel_out, mine, other = call(
        total_kernel,
        "total",
        (shape((KS, RB, 8, W), jnp.float32), columns_half, columns_half),
        (row, selected),
        (parts,),
    )
    others = lax.all_gather(other, "core", axis=0)
    slices = call(
        diag_kernel,
        "diag",
        shape((32, 4, 8, 128), jnp.int16),
        (row,),
        (mine, others, lower, pair),
    )
    slices = lax.all_to_all(slices, ALL, 0, 0, axis_index_groups=plane, tiled=True)
    along = call(plane_kernel, "plane", shape((8, KS, 8, 128), jnp.float32), (), (slices,))
    along = lax.all_to_all(along, ALL, 0, 0, axis_index_groups=line, tiled=True)
    whole = call(line_kernel, "line", shape((32, 4, 8, 128), jnp.int16), (), (along,))
    whole = lax.all_to_all(whole, ALL, 0, 0, axis_index_groups=plane, tiled=True)
    both = lax.all_gather(whole, "core", axis=0)
    diagonal = call(
        finish_kernel, "finish", shape((KS, W, W), jnp.float32), (), (both, diag_inverse)
    )
    return (panel_out[:, :, None], diagonal)


def solution(mesh):
    finer = Mesh(mesh.devices.reshape(4, 2, 2, 2, 4, 4), ROW + COL)
    in_specs = (
        P(None, ROW, None, None, COL, None),
        P(None, None, ROW, COL, None),
        P(),
        P(),
    )
    out_specs = (P(None, None, ROW, COL, None), P())
    return jax.shard_map(
        per_device, mesh=finer, in_specs=in_specs, out_specs=out_specs, check_vma=False
    )
```

```python
import functools

import jax
import jax.numpy as jnp
import numpy as np
from jax import lax
from jax.experimental import pallas as pl
from jax.experimental.pallas import tpu as pltpu
from jax.sharding import Mesh, PartitionSpec as P

KS, RB, W = 3, 4, 256
ROW = ("x", "zh", "core")
COL = ("yh", "yl", "zl")
TARGET = ("yl", "zl", "yh")
ALL = ROW + COL
STEPS = 32760.0
FLOOR = 1e-36
NEAREST = 12582912.0
LIMIT = 24 * 1024 * 1024


def grouped(size, *parts):
    return np.concatenate([part.reshape(-1, size) for part in parts]).tolist()


def groups():
    index = np.arange(512).reshape(4, 2, 2, 8, 4)
    first, second = index[:, :, 0], index[:, :, 1]
    split = second.reshape(4, 2, 4, 2, 4)
    near = grouped(4, first, split.transpose(0, 1, 3, 4, 2))
    far = grouped(8, first.transpose(0, 1, 3, 2), split)
    plane = grouped(32, first.transpose(2, 0, 1, 3), second.transpose(1, 3, 2, 0))
    line = grouped(8, first.transpose(0, 1, 3, 2), second.transpose(0, 2, 1, 3))
    return near, far, plane, line


def coded(block):
    peak = jnp.maximum(jnp.max(jnp.abs(block), axis=-1, keepdims=True), FLOOR)
    code = jnp.ceil(jnp.log2(peak) * 8.0 + 0.01)
    whole = (block * (jnp.exp2(code * -0.125) * STEPS) + NEAREST) - NEAREST
    return whole.astype(jnp.int32).astype(jnp.int16), code


def scale_of(codes):
    return jnp.exp2(codes.astype(jnp.float32) * 0.125) * (1.0 / STEPS)


def spread_kernel(row_ref, selected_ref, lower_ref, out_ref):
    for k in range(KS):
        for s in range(2):
            for h in range(2):
                r = 2 * s + h
                keep = selected_ref[k, r * 16 + row_ref[0]].astype(jnp.float32)
                block = (lower_ref[k, r].astype(jnp.float32) * keep).astype(jnp.bfloat16)
                for chip in range(8):
                    out_ref[chip * 2 + s, h * KS + k] = block


def by_peer(block, core):
    if core == 1:
        return block.reshape(32, 8, 128)
    return block.reshape(8, 4, 8, 128).transpose(1, 0, 2, 3).reshape(32, 8, 128)


def product_kernel(row_ref, pair_ref, tile_ref, cols_ref, out_ref):
    del pair_ref

    def body(core):
        lane = lax.broadcasted_iota(jnp.int32, (W, 128), 1)
        codes = jnp.zeros((W, 128), jnp.float32)
        for k in range(KS):
            halves = []
            for s in range(2):
                part = cols_ref[s, :, k].reshape(16, 2, 8, W)
                halves += [part[:, y].reshape(W // 2, W) for y in range(2)]
            columns = jnp.concatenate(halves, axis=0)
            for r in range(RB):
                block = jnp.dot(
                    tile_ref[r * W : (r + 1) * W, :], columns, preferred_element_type=jnp.float32
                )
                whole, code = coded(block)
                for half in range(2):
                    out_ref[:, r * 6 + k * 2 + half] = by_peer(
                        whole[:, half * 128 : (half + 1) * 128], core
                    )
                codes = jnp.where(lane == r * KS + k, code, codes)
        out_ref[:, 24] = by_peer(codes.astype(jnp.int32).astype(jnp.int16), core)

    for core in range(2):
        pl.when(lax.rem(row_ref[0], 2) == core)(functools.partial(body, core))


def fold_kernel(parts_ref, out_ref):
    scales = scale_of(parts_ref[:, 24])
    lane = lax.broadcasted_iota(jnp.int32, (8, 8, 128), 2)
    codes = jnp.zeros((8, 8, 128), jnp.float32)
    for k in range(KS):
        for r in range(RB):
            at = r * KS + k
            halves = []
            for half in range(2):
                part = parts_ref[:, r * 6 + k * 2 + half].astype(jnp.float32)
                part = part * scales[:, :, at : at + 1]
                halves.append(jnp.sum(part.reshape(4, 8, 8, 128), axis=0))
            whole, code = coded(jnp.concatenate(halves, axis=2))
            for half in range(2):
                out_ref[:, r * 6 + k * 2 + half] = whole[:, :, half * 128 : (half + 1) * 128]
            codes = jnp.where(lane == at, code, codes)
    out_ref[:, 24] = codes.astype(jnp.int32).astype(jnp.int16)


def total_kernel(row_ref, selected_ref, parts_ref, panel_ref, mine_ref, other_ref):
    scales = scale_of(parts_ref[:, 24])
    core = lax.rem(row_ref[0], 2)
    for k in range(KS):
        for r in range(RB):
            keep = selected_ref[k, r * 16 + row_ref[0]].astype(jnp.float32)
            at = r * KS + k
            scale = scales[:, :, at : at + 1]
            halves = []
            for half in range(2):
                part = parts_ref[:, r * 6 + k * 2 + half].astype(jnp.float32)
                halves.append(-(jnp.sum(part * scale, axis=0) * keep))
            panel_ref[k, r] = jnp.concatenate(halves, axis=1)
            mine_ref[k, r] = jnp.where(core == 0, halves[0], halves[1])
            other_ref[k, r] = jnp.where(core == 0, halves[1], halves[0])


def diag_kernel(row_ref, mine_ref, both_ref, lower_ref, pair_ref, out_ref):
    partner = 1 - lax.rem(row_ref[0], 2)
    lane = lax.broadcasted_iota(jnp.int32, (32, 8, 128), 2)
    codes = jnp.zeros((32, 8, 128), jnp.float32)
    for k in range(KS):
        rows = [part.reshape(RB * 8, 128) for part in (mine_ref[k], both_ref[partner, k])]
        rows = jnp.concatenate(rows, axis=0)
        high = rows.astype(jnp.bfloat16)
        rest = rows - high.astype(jnp.float32)
        middle = rest.astype(jnp.bfloat16)
        low = (rest - middle.astype(jnp.float32)).astype(jnp.bfloat16)
        lower = [
            ref[k].astype(jnp.float32).reshape(RB * 8, W).astype(jnp.bfloat16)
            for ref in (lower_ref, pair_ref)
        ]
        diag = lax.dot_general(
            jnp.concatenate(lower * 3, axis=0),
            jnp.concatenate([high, middle, low], axis=0),
            (((0,), (0,)), ((), ())),
            preferred_element_type=jnp.float32,
        )
        whole, code = coded(diag.reshape(32, 8, 128))
        out_ref[:, k] = whole
        codes = jnp.where(lane == k, code, codes)
    out_ref[:, KS] = codes.astype(jnp.int32).astype(jnp.int16)


def plane_kernel(coded_ref, out_ref):
    scales = scale_of(coded_ref[:, KS])
    for k in range(KS):
        total = jnp.sum(coded_ref[:, k].astype(jnp.float32) * scales[:, :, k : k + 1], axis=0)
        for chip in range(8):
            out_ref[chip, k] = total


def line_kernel(sums_ref, out_ref):
    lane = lax.broadcasted_iota(jnp.int32, (8, 128), 1)
    codes = jnp.zeros((8, 128), jnp.float32)
    for k in range(KS):
        whole, code = coded(jnp.sum(sums_ref[:, k], axis=0))
        codes = jnp.where(lane == k, code, codes)
        for chip in range(32):
            out_ref[chip, k] = whole
    codes = codes.astype(jnp.int32).astype(jnp.int16)
    for chip in range(32):
        out_ref[chip, KS] = codes


def finish_kernel(coded_ref, diag_ref, out_ref):
    for half in range(2):
        at = slice(half * 128, (half + 1) * 128)
        scales = scale_of(coded_ref[half, :, KS])
        for k in range(KS):
            total = coded_ref[half, :, k].astype(jnp.float32) * scales[:, :, k : k + 1]
            out_ref[k, :, at] = diag_ref[k, :, at] - total.reshape(W, 128)


def call(kernel, name, shapes, scalars, arrays, limit=LIMIT, early=()):
    vmem, smem = pl.BlockSpec(memory_space=pltpu.VMEM), pl.BlockSpec(memory_space=pltpu.SMEM)
    return pl.pallas_call(
        kernel,
        out_shape=shapes,
        in_specs=[smem] * len(scalars)
        + [pl.BlockSpec(memory_space=pl.ANY)] * len(early)
        + [vmem] * len(arrays),
        out_specs=jax.tree.map(lambda _: vmem, shapes),
        compiler_params=pltpu.CompilerParams(vmem_limit_bytes=limit),
        name=name,
    )(*scalars, *early, *arrays)


def per_device(inverse_tiles, lower_panels, diag_inverse, selected):
    row = lax.axis_index(ROW).astype(jnp.int32).reshape(1)
    near, far, plane, line = groups()
    lower = lower_panels[:, :, 0]
    shape = jax.ShapeDtypeStruct
    pieces = call(
        spread_kernel,
        "spread",
        shape((16, 2 * KS, 8, W), jnp.bfloat16),
        (row, selected),
        (lower,),
        limit=None,
    )
    pieces = lax.all_to_all(pieces, ROW, 0, 0, tiled=True).reshape(32, KS, 8, W)
    pair = lax.ppermute(lower, "core", [(0, 1), (1, 0)])
    half = lax.all_to_all(pieces, TARGET, 0, 0, tiled=True)
    columns = lax.all_gather(half, "core", axis=0)
    tile = inverse_tiles.reshape(RB * W, 2 * W)
    parts = call(
        product_kernel, "product", shape((32, 25, 8, 128), jnp.int16), (row,), (tile, columns), early=(pair,)
    )
    parts = lax.all_to_all(parts, ALL, 0, 0, axis_index_groups=near, tiled=True)
    parts = call(fold_kernel, "fold", shape((8, 25, 8, 128), jnp.int16), (), (parts,))
    parts = lax.all_to_all(parts, ALL, 0, 0, axis_index_groups=far, tiled=True)
    columns_half = shape((KS, RB, 8, 128), jnp.float32)
    panel_out, mine, other = call(
        total_kernel,
        "total",
        (shape((KS, RB, 8, W), jnp.float32), columns_half, columns_half),
        (row, selected),
        (parts,),
    )
    others = lax.all_gather(other, "core", axis=0)
    slices = call(
        diag_kernel,
        "diag",
        shape((32, 4, 8, 128), jnp.int16),
        (row,),
        (mine, others, lower, pair),
    )
    slices = lax.all_to_all(slices, ALL, 0, 0, axis_index_groups=plane, tiled=True)
    along = call(plane_kernel, "plane", shape((8, KS, 8, 128), jnp.float32), (), (slices,))
    along = lax.all_to_all(along, ALL, 0, 0, axis_index_groups=line, tiled=True)
    whole = call(line_kernel, "line", shape((32, 4, 8, 128), jnp.int16), (), (along,))
    whole = lax.all_to_all(whole, ALL, 0, 0, axis_index_groups=plane, tiled=True)
    both = lax.all_gather(whole, "core", axis=0)
    diagonal = call(
        finish_kernel, "finish", shape((KS, W, W), jnp.float32), (), (both, diag_inverse)
    )
    return (panel_out[:, :, None], diagonal)


def solution(mesh):
    finer = Mesh(mesh.devices.reshape(4, 2, 2, 2, 4, 4), ROW + COL)
    in_specs = (
        P(None, ROW, None, None, COL, None),
        P(None, None, ROW, COL, None),
        P(),
        P(),
    )
    out_specs = (P(None, None, ROW, COL, None), P())
    return jax.shard_map(
        per_device, mesh=finer, in_specs=in_specs, out_specs=out_specs, check_vma=False
    )
```

```python
import functools

import jax
import jax.numpy as jnp
import numpy as np
from jax import lax
from jax.experimental import pallas as pl
from jax.experimental.pallas import tpu as pltpu
from jax.sharding import Mesh, PartitionSpec as P

KS, RB, W = 3, 4, 256
ROW = ("x", "zh", "core")
COL = ("yh", "yl", "zl")
TARGET = ("yl", "zl", "yh")
ALL = ROW + COL
STEPS = 32760.0
FLOOR = 1e-36
LIMIT = 24 * 1024 * 1024


def grouped(size, *parts):
    return np.concatenate([part.reshape(-1, size) for part in parts]).tolist()


def groups():
    index = np.arange(512).reshape(4, 2, 2, 8, 4)
    first, second = index[:, :, 0], index[:, :, 1]
    split = second.reshape(4, 2, 4, 2, 4)
    near = grouped(4, first, split.transpose(0, 1, 3, 4, 2))
    far = grouped(8, first.transpose(0, 1, 3, 2), split)
    plane = grouped(32, first.transpose(2, 0, 1, 3), second.transpose(1, 3, 2, 0))
    line = grouped(8, first.transpose(0, 1, 3, 2), second.transpose(0, 2, 1, 3))
    return near, far, plane, line


def coded(block):
    peak = jnp.maximum(jnp.max(jnp.abs(block), axis=-1, keepdims=True), FLOOR)
    code = jnp.ceil(jnp.log2(peak) * 8.0 + 0.01)
    whole = jnp.round(block * (jnp.exp2(code * -0.125) * STEPS))
    return whole.astype(jnp.int32).astype(jnp.int16), code


def scale_of(codes):
    return jnp.exp2(codes.astype(jnp.float32) * 0.125) * (1.0 / STEPS)


def spread_kernel(row_ref, selected_ref, lower_ref, out_ref):
    for k in range(KS):
        for s in range(2):
            for h in range(2):
                r = 2 * s + h
                keep = selected_ref[k, r * 16 + row_ref[0]].astype(jnp.float32)
                block = (lower_ref[k, r].astype(jnp.float32) * keep).astype(jnp.bfloat16)
                for chip in range(8):
                    out_ref[chip * 2 + s, h * KS + k] = block


def by_peer(block, core):
    if core == 1:
        return block.reshape(32, 8, 128)
    return block.reshape(8, 4, 8, 128).transpose(1, 0, 2, 3).reshape(32, 8, 128)


def product_kernel(row_ref, pair_ref, tile_ref, cols_ref, out_ref):
    del pair_ref

    def body(core):
        lane = lax.broadcasted_iota(jnp.int32, (W, 128), 1)
        codes = jnp.zeros((W, 128), jnp.float32)
        for k in range(KS):
            halves = []
            for s in range(2):
                part = cols_ref[s, :, k].reshape(16, 2, 8, W)
                halves += [part[:, y].reshape(W // 2, W) for y in range(2)]
            columns = jnp.concatenate(halves, axis=0)
            for r in range(RB):
                block = jnp.dot(
                    tile_ref[r * W : (r + 1) * W, :], columns, preferred_element_type=jnp.float32
                )
                whole, code = coded(block)
                for half in range(2):
                    out_ref[:, r * 6 + k * 2 + half] = by_peer(
                        whole[:, half * 128 : (half + 1) * 128], core
                    )
                codes = jnp.where(lane == r * KS + k, code, codes)
        out_ref[:, 24] = by_peer(codes.astype(jnp.int32).astype(jnp.int16), core)

    for core in range(2):
        pl.when(lax.rem(row_ref[0], 2) == core)(functools.partial(body, core))


def fold_kernel(parts_ref, out_ref):
    scales = scale_of(parts_ref[:, 24])
    lane = lax.broadcasted_iota(jnp.int32, (8, 8, 128), 2)
    codes = jnp.zeros((8, 8, 128), jnp.float32)
    for k in range(KS):
        for r in range(RB):
            at = r * KS + k
            scale = jnp.broadcast_to(scales[:, :, at : at + 1], scales.shape)
            halves = []
            for half in range(2):
                part = parts_ref[:, r * 6 + k * 2 + half].astype(jnp.float32) * scale
                halves.append(jnp.sum(part.reshape(4, 8, 8, 128), axis=0))
            whole, code = coded(jnp.concatenate(halves, axis=2))
            for half in range(2):
                out_ref[:, r * 6 + k * 2 + half] = whole[:, :, half * 128 : (half + 1) * 128]
            codes = jnp.where(lane == at, code, codes)
    out_ref[:, 24] = codes.astype(jnp.int32).astype(jnp.int16)


def total_kernel(row_ref, selected_ref, parts_ref, panel_ref, mine_ref, other_ref):
    scales = scale_of(parts_ref[:, 24])
    core = lax.rem(row_ref[0], 2)
    for k in range(KS):
        for r in range(RB):
            keep = selected_ref[k, r * 16 + row_ref[0]].astype(jnp.float32)
            at = r * KS + k
            scale = jnp.broadcast_to(scales[:, :, at : at + 1], scales.shape)
            halves = []
            for half in range(2):
                part = parts_ref[:, r * 6 + k * 2 + half].astype(jnp.float32)
                halves.append(-(jnp.sum(part * scale, axis=0) * keep))
            panel_ref[k, r] = jnp.concatenate(halves, axis=1)
            mine_ref[k, r] = jnp.where(core == 0, halves[0], halves[1])
            other_ref[k, r] = jnp.where(core == 0, halves[1], halves[0])


def diag_kernel(row_ref, mine_ref, both_ref, lower_ref, pair_ref, out_ref):
    partner = 1 - lax.rem(row_ref[0], 2)
    lane = lax.broadcasted_iota(jnp.int32, (32, 8, 128), 2)
    codes = jnp.zeros((32, 8, 128), jnp.float32)
    for k in range(KS):
        rows = [part.reshape(RB * 8, 128) for part in (mine_ref[k], both_ref[partner, k])]
        rows = jnp.concatenate(rows, axis=0)
        high = rows.astype(jnp.bfloat16)
        rest = rows - high.astype(jnp.float32)
        middle = rest.astype(jnp.bfloat16)
        low = (rest - middle.astype(jnp.float32)).astype(jnp.bfloat16)
        lower = [
            ref[k].astype(jnp.float32).reshape(RB * 8, W).astype(jnp.bfloat16)
            for ref in (lower_ref, pair_ref)
        ]
        diag = lax.dot_general(
            jnp.concatenate(lower * 3, axis=0),
            jnp.concatenate([high, middle, low], axis=0),
            (((0,), (0,)), ((), ())),
            preferred_element_type=jnp.float32,
        )
        whole, code = coded(diag.reshape(32, 8, 128))
        out_ref[:, k] = whole
        codes = jnp.where(lane == k, code, codes)
    out_ref[:, KS] = codes.astype(jnp.int32).astype(jnp.int16)


def plane_kernel(coded_ref, out_ref):
    scales = scale_of(coded_ref[:, KS])
    for k in range(KS):
        total = jnp.sum(coded_ref[:, k].astype(jnp.float32) * scales[:, :, k : k + 1], axis=0)
        for chip in range(8):
            out_ref[chip, k] = total


def line_kernel(sums_ref, out_ref):
    lane = lax.broadcasted_iota(jnp.int32, (8, 128), 1)
    codes = jnp.zeros((8, 128), jnp.float32)
    for k in range(KS):
        whole, code = coded(jnp.sum(sums_ref[:, k], axis=0))
        codes = jnp.where(lane == k, code, codes)
        for chip in range(32):
            out_ref[chip, k] = whole
    codes = codes.astype(jnp.int32).astype(jnp.int16)
    for chip in range(32):
        out_ref[chip, KS] = codes


def finish_kernel(coded_ref, diag_ref, out_ref):
    for half in range(2):
        at = slice(half * 128, (half + 1) * 128)
        scales = scale_of(coded_ref[half, :, KS])
        for k in range(KS):
            total = coded_ref[half, :, k].astype(jnp.float32) * scales[:, :, k : k + 1]
            out_ref[k, :, at] = diag_ref[k, :, at] - total.reshape(W, 128)


def call(kernel, name, shapes, scalars, arrays, limit=LIMIT, early=()):
    vmem, smem = pl.BlockSpec(memory_space=pltpu.VMEM), pl.BlockSpec(memory_space=pltpu.SMEM)
    return pl.pallas_call(
        kernel,
        out_shape=shapes,
        in_specs=[smem] * len(scalars)
        + [pl.BlockSpec(memory_space=pl.ANY)] * len(early)
        + [vmem] * len(arrays),
        out_specs=jax.tree.map(lambda _: vmem, shapes),
        compiler_params=pltpu.CompilerParams(vmem_limit_bytes=limit),
        name=name,
    )(*scalars, *early, *arrays)


def per_device(inverse_tiles, lower_panels, diag_inverse, selected):
    row = lax.axis_index(ROW).astype(jnp.int32).reshape(1)
    near, far, plane, line = groups()
    lower = lower_panels[:, :, 0]
    shape = jax.ShapeDtypeStruct
    pieces = call(
        spread_kernel,
        "spread",
        shape((16, 2 * KS, 8, W), jnp.bfloat16),
        (row, selected),
        (lower,),
        limit=None,
    )
    pieces = lax.all_to_all(pieces, ROW, 0, 0, tiled=True).reshape(32, KS, 8, W)
    pair = lax.ppermute(lower, "core", [(0, 1), (1, 0)])
    half = lax.all_to_all(pieces, TARGET, 0, 0, tiled=True)
    columns = lax.all_gather(half, "core", axis=0)
    tile = inverse_tiles.reshape(RB * W, 2 * W)
    parts = call(
        product_kernel, "product", shape((32, 25, 8, 128), jnp.int16), (row,), (tile, columns), early=(pair,)
    )
    parts = lax.all_to_all(parts, ALL, 0, 0, axis_index_groups=near, tiled=True)
    parts = call(fold_kernel, "fold", shape((8, 25, 8, 128), jnp.int16), (), (parts,))
    parts = lax.all_to_all(parts, ALL, 0, 0, axis_index_groups=far, tiled=True)
    columns_half = shape((KS, RB, 8, 128), jnp.float32)
    panel_out, mine, other = call(
        total_kernel,
        "total",
        (shape((KS, RB, 8, W), jnp.float32), columns_half, columns_half),
        (row, selected),
        (parts,),
    )
    others = lax.all_gather(other, "core", axis=0)
    slices = call(
        diag_kernel,
        "diag",
        shape((32, 4, 8, 128), jnp.int16),
        (row,),
        (mine, others, lower, pair),
    )
    slices = lax.all_to_all(slices, ALL, 0, 0, axis_index_groups=plane, tiled=True)
    along = call(plane_kernel, "plane", shape((8, KS, 8, 128), jnp.float32), (), (slices,))
    along = lax.all_to_all(along, ALL, 0, 0, axis_index_groups=line, tiled=True)
    whole = call(line_kernel, "line", shape((32, 4, 8, 128), jnp.int16), (), (along,))
    whole = lax.all_to_all(whole, ALL, 0, 0, axis_index_groups=plane, tiled=True)
    both = lax.all_gather(whole, "core", axis=0)
    diagonal = call(
        finish_kernel, "finish", shape((KS, W, W), jnp.float32), (), (both, diag_inverse)
    )
    return (panel_out[:, :, None], diagonal)


def solution(mesh):
    finer = Mesh(mesh.devices.reshape(4, 2, 2, 2, 4, 4), ROW + COL)
    in_specs = (
        P(None, ROW, None, None, COL, None),
        P(None, None, ROW, COL, None),
        P(),
        P(),
    )
    out_specs = (P(None, None, ROW, COL, None), P())
    return jax.shard_map(
        per_device, mesh=finer, in_specs=in_specs, out_specs=out_specs, check_vma=False
    )
```
